32 devices in a mesh: groups: 2 (over x), expert: 8 (over z, y), wave: 2 (over core).
Axes of the slice: x: 2, y: 2, z: 4, core: 2. Of those that a mesh axis runs over, the one named last changes fastest.
Arguments:
- hidden_rows: bfloat16 [512, 2, 2048], P(('groups', 'expert', 'wave')), parts along dimension 0, may hold values from -6 to 6
- expert_ids: int32 [512, 2, 8], P(('groups', 'expert', 'wave')), parts along dimension 0, may hold values from 0 to 15, all different within a row; in each aligned block of 32 rows (0 to 31, 32 to 63, ..., all dimensions but the last counted through in order) at most 24 rows name the same one
- route_weights: float32 [512, 2, 8], P(('groups', 'expert', 'wave')), parts along dimension 0, may hold values from 0.1 to 1
- w_gate: bfloat16 [16, 2048, 768], P('expert', None, 'wave'), may hold values from -0.125 to 0.125
- w_up: bfloat16 [16, 2048, 768], P('expert', None, 'wave'), may hold values from -0.125 to 0.125
- w_down: bfloat16 [16, 768, 2048], P('expert', 'wave'), may hold values from -0.21875 to 0.21875
- codes: int32 [512, 2, 16], P(('groups', 'expert', 'wave')), parts along dimension 0, may hold values from 0 to 1023
- owner_slot: int32 [512], P(('groups', 'expert', 'wave')), parts along dimension 0, may hold values from 0 to 255, as said below
- code_table: bfloat16 [16, 1024, 1024], P(None, 'expert'), may hold values from -1.5 to 1.5
- conv_state: bfloat16 [512, 6, 1024], P(('groups', 'expert', 'wave')), parts along dimension 0, may hold values from -6 to 6
- conv_taps: float32 [7, 1024], replicated, may hold values from -2.4 to 2.4
- conv_bias: float32 [1024], replicated, may hold values from -3 to 3
- upsample: bfloat16 [1024, 512], replicated, may hold values from -0.1875 to 0.1875
Outputs:
- moe_out: bfloat16 [512, 2, 2048], P(('groups', 'expert', 'wave')), parts along dimension 0
- waveform: bfloat16 [512, 2, 512], P(('groups', 'expert', 'wave')), parts along dimension 0
- new_state: bfloat16 [512, 6, 1024], P(('groups', 'expert', 'wave')), parts along dimension 0
The draws below stay inside these ranges and needn't reach their ends.
There are 2 independent parts, one for each index of `groups`. The reference program is written for one: setup_inputs(seed, part) draws one part's arguments, and reference() takes and returns one part's arrays. A program takes and returns all parts, laid end to end along the dimension named above; an argument that names none is the same for every part. Nothing has to cross between parts.
Inputs may be any that keep to these rules, and one draw needn't show every extreme that they name: `expert_ids`: each row names 8 different experts; among the 32 rows of one device no expert is named more than 24 times, a bound that some block reaches. `owner_slot`: A permutation of the slots. Slot o lies on the device holding rows o of the decoder's arrays; a session's slot lies on a device with the same index along wave as the session's own device, so every device holds 16 slots.
All inputs are finite; a program needn't handle non-finite values.
Results may differ from the reference program's by a relative error of at most 0.012.
Values may be sent and summed in bfloat16 or wider, within the bound.
A program may use at most 64 MiB of HBM per device.

```python
import math
import jax
import jax.numpy as jnp
import numpy as np
from jax import lax

D = 2048
FF = 768
TOP = 8
STEPS = 2
SESS_DEV = 16
CODEBOOKS = 16
CODES = 1024
DC = 1024
KERNEL = 7
UP = 2
OUT_CH = 256
EXPERTS = 16
CAP = 24
SESSIONS = 256
STATE = 6
N_EXPERT = 8
N_WAVE = 2


def draw_owner_slot(key, part):
    count = SESSIONS // N_WAVE
    owners = jnp.zeros((SESSIONS,), jnp.int32)
    within = jnp.arange(count, dtype=jnp.int32)
    for wave_index in range(N_WAVE):
        order = jax.random.permutation(jax.random.fold_in(key, 11 + wave_index), count).astype(jnp.int32)
        where = (within // SESS_DEV * N_WAVE + wave_index) * SESS_DEV + within % SESS_DEV
        target = (order // SESS_DEV * N_WAVE + wave_index) * SESS_DEV + order % SESS_DEV
        owners = owners.at[where].set(target)
    return owners


def place_ends(values, rng, smallest, largest):
    extent = values.shape
    place = [jax.random.randint(jax.random.fold_in(rng, axis), (), 0, extent[axis]) for axis in range(len(extent))]
    values = values.at[tuple(place)].set(smallest)
    longest = extent.index(max(extent))
    place[longest] = (place[longest] + 1) % extent[longest]
    return values.at[tuple(place)].set(largest)


def block_scale(own_key, dims, shards, least, top_value):
    level = 1.0
    for dim, parts in shards:
        draws = jax.random.uniform(jax.random.fold_in(jax.random.fold_in(own_key, 6), dim), (parts,), jnp.float32, least / len(shards), top_value / len(shards))
        level = level * jnp.repeat(jnp.exp(draws), dims[dim] // parts).reshape((-1,) + (1,) * (len(dims) - 1 - dim))
    return level


def shared_out(rng, own, number, rows, amount, top, limit, lean):
    sequence = jax.random.permutation(rng, amount)
    crowded, ordinary = shares(amount, rows * top, limit, lean, True), shares(amount, rows * top, limit, lean, False)
    places = jnp.arange(amount)

    def named(sizes, offset_by):
        used = int((sizes > 0).sum())
        fixed = max(1, used // 4)
        passed = fixed + (places - fixed + offset_by * (used - fixed)) % max(1, amount - fixed)
        return jnp.zeros((amount,), jnp.int32).at[sequence[jnp.where(places < fixed, places, passed)]].set(jnp.asarray(sizes, jnp.int32))

    sizes = jnp.where(number % 4 == 0, named(crowded, number // 4), named(ordinary, number - number // 4 - 1))
    mixed = jax.random.permutation(jax.random.fold_in(own, 3), amount)
    source_of, taker = mixed[0:amount // 2 * 2:2], mixed[1:amount // 2 * 2:2]
    room = jnp.minimum(sizes[source_of] - 1, limit - sizes[taker]) // 2
    room = jnp.where((source_of == sequence[0]) | (taker == sequence[0]) | (sizes[taker] == 0), 0, jnp.maximum(room, 0))
    passed = jax.random.randint(jax.random.fold_in(own, 4), (amount // 2,), 0, 1 << 20) % (room + 1)
    sizes = sizes.at[source_of].add(-passed).at[taker].add(passed)
    members = jnp.searchsorted(jnp.cumsum(sizes), jnp.arange(rows * top), side="right").astype(jnp.int32)
    grid = members.reshape(top, rows).T
    grid = grid[jax.random.permutation(jax.random.fold_in(own, 1), rows)]
    offset_by = jax.random.randint(jax.random.fold_in(own, 2), (rows, 1), 0, top)
    return jnp.take_along_axis(grid, (jnp.arange(top)[None, :] + offset_by) % top, axis=1)


def shares(count, total, bound, skew, full):
    portions = [(1 << 20) // math.isqrt(standing ** skew) + 1 for standing in range(1, count + 1)]
    largest = bound if full else min(bound, max(-(-total // count), total * portions[0] // sum(portions)))
    least = 1 if total - largest >= count - 1 else 0
    given, surplus = [largest] + [least] * (count - 1), total - largest - least * (count - 1)
    while surplus > 0:
        movable = [i for i in range(1, count) if given[i] < largest] or [i for i in range(1, count) if given[i] < bound]
        pool, budget = sum([portions[i] for i in movable]), surplus
        for i in movable:
            extra = min(bound - given[i], max(1, budget * portions[i] // pool), surplus)
            given[i] = given[i] + extra
            surplus = surplus - extra
    return np.array(given)


def centred(stream_key, extent, deviation, bound, split=(), held_as=jnp.bfloat16):
    values = jax.random.normal(stream_key, extent, jnp.float32) * deviation
    if len(split) > 0:
        values = block_scale(stream_key, extent, split, -0.22, 0.18) * values
    return jnp.clip(values, min=-bound, max=bound).astype(held_as)


def setup_inputs(seed: int = 0, part: int = 0) -> dict:
    arg_keys = jax.random.split(jax.random.key(seed), 14)
    part_splits = jax.random.split(jax.random.fold_in(arg_keys[13], part), 14)
    hidden_rows = centred(part_splits[0], (SESSIONS, STEPS, D), 1.0, 6.0, ((0, 16),))
    expert_ids_keys = jax.random.split(jax.random.fold_in(part_splits[1], 1), SESSIONS * STEPS // (SESS_DEV * STEPS))
    expert_ids_turns = jax.random.permutation(jax.random.fold_in(part_splits[1], 3), SESSIONS * STEPS // (SESS_DEV * STEPS))
    expert_ids = jax.vmap(lambda own, number: shared_out(jax.random.fold_in(part_splits[1], 2), own, number, SESS_DEV * STEPS, EXPERTS, TOP, CAP, 1))(expert_ids_keys, expert_ids_turns).reshape((SESSIONS, STEPS, TOP))
    route_weights = jnp.clip(jnp.exp(math.log(1.0) - 2.3025851 * jax.random.uniform(part_splits[2], (SESSIONS, STEPS, TOP), jnp.float32) ** block_scale(part_splits[2], (SESSIONS, STEPS, TOP), ((0, 16),), -0.2, 0.2)), 0.1, 1.0)
    w_gate = centred(arg_keys[3], (EXPERTS, D, FF), D ** -0.5, 0.125, ((0, 8), (2, 2)))
    w_up = centred(arg_keys[4], (EXPERTS, D, FF), D ** -0.5, 0.125, ((0, 8), (2, 2)))
    w_down = centred(arg_keys[5], (EXPERTS, FF, D), FF ** -0.5, 0.21875, ((0, 8), (1, 2)))
    codes = place_ends(jax.random.randint(part_splits[6], (SESSIONS, STEPS, CODEBOOKS), 0, CODES), jax.random.fold_in(part_splits[6], 1), 0, CODES - 1).astype(jnp.int32)
    owner_slot = draw_owner_slot(jax.random.fold_in(jax.random.fold_in(arg_keys[13], part), 71), part)
    code_table = centred(arg_keys[8], (CODEBOOKS, CODES, DC), 0.25, 1.5, ((1, 8),))
    conv_state = centred(part_splits[9], (SESSIONS, STATE, DC), 1.0, 6.0, ((0, 16),))
    conv_taps = centred(arg_keys[10], (KERNEL, DC), 0.4, 2.4, (), jnp.float32)
    conv_bias = centred(arg_keys[11], (DC,), 0.5, 3.0, (), jnp.float32)
    upsample = centred(arg_keys[12], (DC, UP * OUT_CH), DC ** -0.5, 0.1875)
    return dict(hidden_rows=hidden_rows, expert_ids=expert_ids, route_weights=route_weights, w_gate=w_gate, w_up=w_up, w_down=w_down, codes=codes, owner_slot=owner_slot, code_table=code_table, conv_state=conv_state, conv_taps=conv_taps, conv_bias=conv_bias, upsample=upsample)


def round_half(value):
    return lax.optimization_barrier(value.astype(jnp.bfloat16)).astype(jnp.float32)


def reference(hidden_rows, expert_ids, route_weights, w_gate, w_up, w_down, codes, owner_slot, code_table, conv_state, conv_taps, conv_bias, upsample):
    row_total = SESSIONS * STEPS
    tok_rows = hidden_rows.reshape(row_total, D)
    chosen = expert_ids.reshape(row_total * TOP).astype(jnp.int32)
    weights_flat = route_weights.reshape(row_total * TOP)
    most = N_EXPERT * N_WAVE * CAP
    group_width = FF // N_WAVE

    def one_expert(total, index):
        hit = chosen == index
        picked = jnp.nonzero(hit, size=most, fill_value=0)[0].astype(jnp.int32)
        valid = (jnp.arange(most, dtype=jnp.int32) < jnp.sum(hit.astype(jnp.int32))).astype(jnp.float32)
        source = picked // TOP
        inputs = tok_rows[source]
        gate_val = jnp.dot(inputs, w_gate[index], preferred_element_type=jnp.float32)
        up_val = jnp.dot(inputs, w_up[index], preferred_element_type=jnp.float32)
        activated = (jax.nn.silu(gate_val) * up_val).astype(jnp.bfloat16)
        down_rows = w_down[index]
        summed = jnp.zeros((most, D), jnp.float32)
        for group in range(N_WAVE):
            term = jnp.dot(activated[:, group * group_width:(group + 1) * group_width], down_rows[group * group_width:(group + 1) * group_width], preferred_element_type=jnp.float32)
            summed = summed + round_half(term)
        slot_out = round_half(summed)
        total = total.at[source].add(slot_out * (weights_flat[picked] * valid)[:, None])
        return total, None

    mixed, _ = lax.scan(one_expert, jnp.zeros((row_total, D), jnp.float32), jnp.arange(EXPERTS, dtype=jnp.int32))
    moe_out = mixed.astype(jnp.bfloat16).reshape(SESSIONS, STEPS, D)

    books = jnp.arange(CODEBOOKS, dtype=jnp.int32)
    looked = code_table[books[None, None, :], codes].astype(jnp.float32)
    frames = jnp.sum(looked, axis=2)
    owned = jnp.zeros((SESSIONS, STEPS, DC), jnp.float32).at[owner_slot].set(frames)
    history = jnp.concatenate([conv_state.astype(jnp.float32), owned], axis=1)
    filtered = jnp.broadcast_to(conv_bias, (SESSIONS, STEPS, DC))
    for offset in range(KERNEL):
        filtered = filtered + conv_taps[offset] * history[:, STATE - offset:STATE - offset + STEPS]
    decoded = jax.nn.gelu(filtered).astype(jnp.bfloat16)
    samples = jnp.dot(decoded.reshape(SESSIONS * STEPS, DC), upsample, preferred_element_type=jnp.float32)
    waveform = samples.astype(jnp.bfloat16).reshape(SESSIONS, STEPS, UP * OUT_CH)
    new_state = history[:, STEPS:].astype(jnp.bfloat16)
    return (moe_out, waveform, new_state)
```

```python
import functools

import jax
import jax.numpy as jnp
from jax import lax
from jax.experimental import pallas as pl
from jax.experimental.pallas import tpu as pltpu
from jax.sharding import PartitionSpec as P

MESH = pl.DeviceIdType.MESH
BF = jnp.bfloat16
F32 = jnp.float32
RADIX = 64
LANES = 128
INNER = 2
HALVES = 2


def dot(a, b):
    return jnp.dot(a, b, preferred_element_type=F32)


def kernel(
    n_e, experts, books,
    h_ref, id_ref, rw_ref, co_ref, ow_ref, st_ref, tap_ref, bias_ref, us_ref,
    wg_ref, wu_ref, wd_ref, tab_ref,
    moe_ref, wave_ref, new_ref,
    hv, idv, rwv, cov, owv, stv, tapv, biasv, usv,
    xg, meta, wgu, wdv, tabv, mem, act, early, told, po, pn, my, ma, mz,
    fs, fy, fa, fz, fr,
    in_sem, w_sem, pws, pwr, zus, zds, yss, agr, mes, mer,
    mys, myr, mzs, mzr, fys, fyr, fzs, fzr,
):
    outer = n_e // INNER
    sessions, steps, width = hv.shape
    rows = sessions * steps
    channels = tab_ref.shape[1]
    local, _, units = wg_ref.shape
    ff = 2 * units
    shard = tab_ref.shape[0] // books
    wave_rows = n_e * rows
    col_rows = outer * rows
    e = lax.axis_index("expert")
    w = lax.axis_index("wave")
    z = e // INNER
    y = e % INNER
    peer = 1 - w
    ye = z * INNER + (1 - y)
    low = z < outer // 2

    def remote(src, dst, ssem, rsem, te, tw):
        return pltpu.make_async_remote_copy(
            src_ref=src, dst_ref=dst, send_sem=ssem, recv_sem=rsem,
            device_id={"expert": te, "wave": tw}, device_id_type=MESH,
        )

    barrier = pltpu.get_barrier_semaphore()

    def greet(te, tw):
        pl.semaphore_signal(barrier, inc=1, device_id={"expert": te, "wave": tw}, device_id_type=MESH)

    greet(e, peer)
    for d in range(1, n_e):
        greet((e + d) % n_e, w)

    firsts = [
        pltpu.make_async_copy(src, dst, in_sem.at[i])
        for i, (src, dst) in enumerate((
            (h_ref, hv), (id_ref, idv), (rw_ref, rwv), (co_ref, cov), (ow_ref, owv),
            (st_ref, stv), (tap_ref, tapv), (bias_ref, biasv), (us_ref, usv),
        ))
    ]
    for copy in firsts[:5]:
        copy.start()

    def gate_at(tw):
        return pl.ds(pl.multiple_of(tw * units, LANES), units)

    def up_at(tw):
        return pl.ds(pl.multiple_of(ff + tw * units, LANES), units)

    def down_at(j, tw):
        return pl.ds(pl.multiple_of(j * ff + tw * units, LANES), units)

    def weights(tw):
        pairs = []
        for j in range(local):
            pairs.append((wg_ref.at[j], wgu.at[j, :, gate_at(tw)]))
            pairs.append((wu_ref.at[j], wgu.at[j, :, up_at(tw)]))
        for j in range(local):
            pairs.append((wd_ref.at[pl.ds(j * units, units), :], wdv.at[down_at(j, tw), :]))
        return pairs

    loads = [
        pltpu.make_async_copy(src, dst, w_sem.at[i]) for i, (src, dst) in enumerate(weights(w))
    ]
    table = pltpu.make_async_copy(tab_ref, tabv, w_sem.at[3 * local])
    gives = [
        remote(src, dst, pws.at[i], pwr.at[i], e, peer) for i, (src, dst) in enumerate(weights(w))
    ]
    takes = [
        remote(src, dst, pws.at[i], pwr.at[i], e, peer) for i, (src, dst) in enumerate(weights(peer))
    ]

    half = rows // HALVES

    def at(rel, zo, p):
        return pl.ds(pl.multiple_of((rel * outer + zo) * rows + p * half, half), half)

    def agsem(rel, zo, p):
        return agr.at[(rel * outer + zo) * HALVES + p]

    def up(zo, p):
        s = xg.at[at(0, zo, p), :]
        return remote(s, s, zus.at[zo * HALVES + p], agsem(0, zo, p), (z + 1) * INNER + y, w)

    def down(zo, p):
        s = xg.at[at(0, zo, p), :]
        return remote(s, s, zds.at[zo * HALVES + p], agsem(0, zo, p), (z - 1) * INNER + y, w)

    def across(zo, p):
        return remote(
            xg.at[at(0, zo, p), :], xg.at[at(1, zo, p), :], yss.at[zo * HALVES + p], agsem(1, zo, p), ye, w
        )

    def arrived(rel, zo, p):
        s = xg.at[at(rel, zo, p), :]
        remote(s, s, yss.at[0], agsem(rel, zo, p), ye, w).wait_recv()

    def meta_at(te, se):
        rel = (te % INNER + se % INNER) % 2
        return pl.ds(pl.multiple_of((rel * outer + se // INNER) * rows, rows), rows)

    def tell(d):
        te = (e + d) % n_e
        return remote(
            meta.at[meta_at(e, e), :], meta.at[meta_at(te, e), :], mes.at[d - 1], mer.at[d - 1], te, w
        )

    def told_by(d):
        se = (e - d + n_e) % n_e
        s = meta.at[meta_at(e, se), :]
        return remote(s, s, mes.at[d - 1], mer.at[d - 1], se, w)

    firsts[0].wait()
    hid = hv[...]
    mine_at = pl.multiple_of(z * rows, rows)
    for t in range(steps):
        xg[pl.ds(mine_at + t * sessions, sessions), :] = hid[:, t, :]
    for copy in firsts[5:]:
        copy.start()
    table.start()
    for load in loads:
        load.start()
    pl.semaphore_wait(barrier, n_e)

    for p in range(HALVES):
        @pl.when(z + 1 < outer)
        def _():
            up(z, p).start()

        @pl.when(z > 0)
        def _():
            down(z, p).start()

        across(z, p).start()
    for give in gives:
        give.start()

    lanes = meta.shape[1]
    code_at = 2 * experts
    dest_at = code_at + 2 * books
    lane_i = lax.broadcasted_iota(jnp.int32, (sessions, lanes), 1)
    eye = lax.broadcasted_iota(jnp.int32, (sessions, sessions), 0) == lax.broadcasted_iota(
        jnp.int32, (sessions, sessions), 1
    )
    lane_f = lane_i.astype(F32)

    def column(row):
        square = jnp.broadcast_to(row.astype(F32), (sessions, sessions))
        return jnp.sum(jnp.where(eye, square, 0.0), axis=1, keepdims=True)

    for copy in firsts[1:5]:
        copy.wait()
    owner = column(owv[...])
    holder = jnp.floor((owner + 0.5) / sessions)
    within = owner - holder * sessions
    holder = jnp.floor((holder + 0.5) / 2)
    for t in range(steps):
        co = cov[:, t, :].astype(F32)
        both = jnp.zeros((sessions, lanes), F32)
        for k in range(idv.shape[1]):
            named = column(idv[t, k:k + 1, :])
            both += jnp.where(
                (named == lane_f) | (named + experts == lane_f), column(rwv[t, k:k + 1, :]), 0.0
            )
        high = both.astype(BF).astype(F32)
        extra = jnp.where(lane_i < experts, high, both - high)
        extra = jnp.where(lane_i < code_at, extra, 0.0)
        for q in range(books):
            c = co[:, q:q + 1]
            top = jnp.floor((c + 0.5) / RADIX)
            extra = jnp.where(lane_i == code_at + q, top, extra)
            extra = jnp.where(lane_i == code_at + books + q, c - top * RADIX, extra)
        dest = holder * rows + t * sessions + within
        top = jnp.floor((dest + 0.5) / RADIX)
        extra = jnp.where(lane_i == dest_at, top, extra)
        extra = jnp.where(lane_i == dest_at + 1, dest - top * RADIX, extra)
        meta[pl.ds(mine_at + t * sessions, sessions), :] = extra.astype(BF)
    for d in range(1, n_e):
        tell(d).start()

    for copy in firsts[5:]:
        copy.wait()
    state_len = stv.shape[0]
    taps = tapv.shape[0]

    def before():
        for t in range(steps):
            total = jnp.broadcast_to(biasv[...], (sessions, channels))
            for j in range(t + 1, taps):
                total += tapv[j:j + 1, :] * stv[state_len + t - j].astype(F32)
            early[t * sessions:(t + 1) * sessions, :] = total
        for i in range(state_len - steps):
            new_ref[i] = stv[i + steps]

    def forward(step):
        for p in range(HALVES):
            @pl.when(z - step >= 0)
            def _():
                zo = z - step
                arrived(0, zo, p)

                @pl.when(z + 1 < outer)
                def _():
                    up(zo, p).start()

                across(zo, p).start()

            @pl.when(z + step < outer)
            def _():
                zo = z + step
                arrived(0, zo, p)

                @pl.when(z > 0)
                def _():
                    down(zo, p).start()

                across(zo, p).start()

    src = lax.broadcasted_iota(jnp.int32, (lanes, LANES), 0)
    col = lax.broadcasted_iota(jnp.int32, (lanes, LANES), 1)

    def learn():
        for d in range(1, n_e):
            told_by(d).wait_recv()
        is_code = col < books
        pick = jnp.where(is_code & (src == code_at + col), float(RADIX), 0.0)
        pick += jnp.where(is_code & (src == code_at + books + col), 1.0, 0.0)
        pick += jnp.where((col == books) & (src == dest_at), float(RADIX), 0.0)
        pick += jnp.where((col == books) & (src == dest_at + 1), 1.0, 0.0)
        own = e * local + col - (books + 1)
        is_weight = (col > books) & (col <= books + local)
        pick += jnp.where(is_weight & ((src == own) | (src == own + experts)), 1.0, 0.0)
        told[...] = dot(meta[...], pick.astype(BF))
        lane = lax.broadcasted_iota(jnp.int32, (wave_rows, shard), 1).astype(F32)
        first = (e * shard).astype(F32)
        for q in range(books):
            mem[:, q * shard:(q + 1) * shard] = jnp.where(
                told[:, q:q + 1] - first == lane, 1.0, 0.0
            ).astype(BF)

    def embed():
        place = lax.broadcasted_iota(jnp.int32, (wave_rows, wave_rows), 1).astype(F32)
        order = jnp.where(told[:, books:books + 1] == place, 1.0, 0.0).astype(BF)
        table.wait()
        f_tile = min(channels, 512)

        @pl.loop(0, channels // f_tile)
        def _(n):
            cols = pl.ds(pl.multiple_of(n * f_tile, f_tile), f_tile)
            part = dot(mem[...], tabv[:, cols]).astype(BF)
            fs[:, cols] = lax.dot_general(
                order, part, (((0,), (0,)), ((), ())), preferred_element_type=F32
            ).astype(BF)

    def goal(k):
        if k == outer - 1:
            return z
        down_from = outer - 1 - k
        down_from = down_from - (down_from <= z).astype(jnp.int32)
        up_from = k + (k >= z).astype(jnp.int32)
        return jnp.where(low, down_from, up_from)

    def block(zo, yo):
        return pl.ds(pl.multiple_of((zo * INNER + yo) * rows, rows), rows)

    def zrows(zo):
        return pl.ds(pl.multiple_of(zo * rows, rows), rows)

    def hop(zo):
        return (zo - z + outer) % outer - 1

    def fy_copy(zo):
        return remote(fs.at[block(zo, 1 - y), :], fy.at[zrows(zo), :], fys.at[zo], fyr.at[zo], ye, w)

    def fz_copy(zo):
        d = hop(zo)
        return remote(fa.at[zrows(zo), :], fz.at[zrows(d), :], fzs.at[d], fzr.at[d], zo * INNER + y, w)

    def fz_got(d):
        s = fz.at[zrows(d), :]
        return remote(s, s, fzs.at[d], fzr.at[d], ye, w)

    part_cols = width // HALVES

    def cols_of(p):
        return pl.ds(p * part_cols, part_cols)

    def my_copy(zo, p):
        i = zo * HALVES + p
        return remote(
            pn.at[zrows(zo), cols_of(p)], my.at[zrows(zo), cols_of(p)], mys.at[i], myr.at[i], ye, w
        )

    def mz_copy(zo, p):
        d = hop(zo)
        i = d * HALVES + p
        return remote(
            ma.at[zrows(zo), cols_of(p)], mz.at[zrows(d), cols_of(p)], mzs.at[i], mzr.at[i], zo * INNER + y, w
        )

    def mz_got(d, p):
        i = d * HALVES + p
        s = mz.at[zrows(d), cols_of(p)]
        return remote(s, s, mzs.at[i], mzr.at[i], ye, w)

    rc = min(col_rows, 128)

    def looped(count, body):
        if count == 1:
            body(0)
        else:
            pl.loop(0, count)(body)

    def hidden(rel):
        def piece(i):
            here = pl.ds(pl.multiple_of(rel * col_rows + i * rc, rc), rc)
            there = pl.ds(pl.multiple_of(i * rc, rc), rc)
            x = xg[here, :]
            tile = ff // 3 if ff % (3 * LANES) == 0 else ff
            for j in range(local):
                weight = told[here, books + 1 + j:books + 2 + j]
                for n in range(0, ff, tile):
                    g = dot(x, wgu[j, :, n:n + tile])
                    u = dot(x, wgu[j, :, ff + n:ff + n + tile])
                    a = g / (1.0 + jnp.exp(-g)) * u * weight
                    act[there, j * ff + n:j * ff + n + tile] = a.astype(BF)

        looped(col_rows // rc, piece)

    def project(dst, p):
        def piece(i):
            there = pl.ds(pl.multiple_of(i * rc, rc), rc)
            tile = min(part_cols, 512)
            for n in range(p * part_cols, (p + 1) * part_cols, tile):
                dst[there, n:n + tile] = dot(act[there, :], wdv[:, n:n + tile]).astype(BF)

        looped(col_rows // rc, piece)

    before()
    for step in range(1, outer):
        forward(step)
        if step == 1:
            learn()
        if step == min(2, outer - 1):
            embed()
    for k in range(outer):
        fy_copy(goal(k)).start()

    for load in loads:
        load.wait()
    for take in takes:
        take.wait_recv()
    hidden(0)
    for p in range(HALVES):
        project(po, p)
    for zo in range(outer):
        for p in range(HALVES):
            arrived(1, zo, p)
    hidden(1)
    for p in range(HALVES):
        project(pn, p)
        for k in range(outer - 1):
            my_copy(goal(k), p).start()
    for p in range(HALVES):
        my_copy(z, p).start()

    for k in range(outer):
        zo = goal(k)
        total = fs[block(zo, y), :].astype(F32)
        fy_copy(zo).wait_recv()
        total += fy[zrows(zo), :].astype(F32)
        if k < outer - 1:
            fa[zrows(zo), :] = total.astype(BF)
            fz_copy(zo).start()
        else:
            fr[...] = total

    def pass_on(p):
        for k in range(outer - 1):
            zo = goal(k)
            my_copy(zo, p).wait_recv()
            ma[zrows(zo), cols_of(p)] = (
                po[zrows(zo), cols_of(p)].astype(F32) + my[zrows(zo), cols_of(p)].astype(F32)
            ).astype(BF)
            mz_copy(zo, p).start()

    def finish_frames():
        for d in range(outer - 1):
            fz_got(d).wait_recv()
            fr[...] += fz[zrows(d), :].astype(F32)
        got = [fr[t * sessions:(t + 1) * sessions, :] for t in range(steps)]
        decoded = []
        for t in range(steps):
            total = early[t * sessions:(t + 1) * sessions, :]
            for j in range(t + 1):
                total += tapv[j:j + 1, :] * got[t - j]
            decoded.append(jax.nn.gelu(total).astype(BF))
            new_ref[state_len - steps + t] = got[t].astype(BF)
        samples = dot(jnp.concatenate(decoded, axis=0), usv[...]).astype(BF)
        for t in range(steps):
            wave_ref[:, t, :] = samples[t * sessions:(t + 1) * sessions]

    pass_on(0)
    finish_frames()
    for p in range(1, HALVES):
        pass_on(p)
    for p in range(HALVES):
        my_copy(z, p).wait_recv()
        mine = po[zrows(z), cols_of(p)].astype(F32) + my[zrows(z), cols_of(p)].astype(F32)
        for d in range(outer - 1):
            mz_got(d, p).wait_recv()
            mine += mz[zrows(d), cols_of(p)].astype(F32)
        for t in range(steps):
            moe_ref[:, t, p * part_cols:(p + 1) * part_cols] = mine[t * sessions:(t + 1) * sessions].astype(BF)

    for give in gives:
        give.wait_send()
    for d in range(1, n_e):
        tell(d).wait_send()
    for zo in range(outer):
        for p in range(HALVES):
            @pl.when((z + 1 < outer) & (zo <= z))
            def _():
                up(zo, p).wait_send()

            @pl.when((z > 0) & (zo >= z))
            def _():
                down(zo, p).wait_send()

            across(zo, p).wait_send()
            my_copy(zo, p).wait_send()
        fy_copy(zo).wait_send()
    for k in range(outer - 1):
        zo = goal(k)
        fz_copy(zo).wait_send()
        for p in range(HALVES):
            mz_copy(zo, p).wait_send()


def hand_over(a_ref, b_ref, c_ref, a_out, b_out, c_out):
    a_out[...] = a_ref[...]
    b_out[...] = b_ref[...]
    c_out[...] = c_ref[...]


def exchange(args, w_gate, w_up, w_down, table, experts, books):
    n_e = lax.axis_size("expert")
    outer = n_e // INNER
    sessions, steps, width = args[0].shape
    rows = sessions * steps
    used = 2 * experts + 2 * books + 2
    lanes = used + -used % LANES
    local, _, units = w_gate.shape
    ff = 2 * units
    channels = table.shape[1]
    wave_rows = n_e * rows
    col_rows = outer * rows
    vm = pltpu.VMEM
    dma = lambda *s: pltpu.SemaphoreType.DMA(s)
    hops = outer - 1
    scratch = [vm(a.shape, a.dtype) for a in args] + [
        vm((wave_rows, width), BF),
        vm((wave_rows, lanes), BF),
        vm((local, width, 2 * ff), BF),
        vm((local * ff, width), BF),
        vm(table.shape, BF),
        vm((wave_rows, table.shape[0]), BF),
        vm((col_rows, local * ff), BF),
        vm((rows, channels), F32),
        vm((wave_rows, LANES), F32),
        vm((col_rows, width), BF),
        vm((col_rows, width), BF),
        vm((col_rows, width), BF),
        vm((col_rows, width), BF),
        vm((hops * rows, width), BF),
        vm((wave_rows, channels), BF),
        vm((col_rows, channels), BF),
        vm((col_rows, channels), BF),
        vm((hops * rows, channels), BF),
        vm((rows, channels), F32),
        dma(len(args)), dma(3 * local + 1), dma(3 * local), dma(3 * local),
        dma(outer * HALVES), dma(outer * HALVES), dma(outer * HALVES), dma(n_e * HALVES),
        dma(n_e - 1), dma(n_e - 1),
        dma(outer * HALVES), dma(outer * HALVES), dma(hops * HALVES), dma(hops * HALVES),
        dma(outer), dma(outer), dma(hops), dma(hops),
    ]
    any_spec = pl.BlockSpec(memory_space=pl.ANY)
    vm_spec = pl.BlockSpec(memory_space=pltpu.VMEM)
    return pl.pallas_call(
        functools.partial(kernel, n_e, experts, books),
        out_shape=(
            jax.ShapeDtypeStruct((sessions, steps, width), BF),
            jax.ShapeDtypeStruct((sessions, steps, args[8].shape[1]), BF),
            jax.ShapeDtypeStruct(args[5].shape, BF),
        ),
        in_specs=[any_spec] * (len(args) + 4),
        out_specs=(vm_spec, vm_spec, vm_spec),
        scratch_shapes=scratch,
        compiler_params=pltpu.CompilerParams(
            collective_id=0, has_side_effects=True, vmem_limit_bytes=60 * 1024 * 1024
        ),
    )(*args, w_gate, w_up, w_down, table)


def per_device(
    hidden_rows, expert_ids, route_weights, w_gate, w_up, w_down,
    codes, owner_slot, code_table, conv_state, conv_taps, conv_bias, upsample,
):
    n_e = lax.axis_size("expert")
    width = hidden_rows.shape[2]
    experts = n_e * w_gate.shape[0]
    books, shard, channels = code_table.shape
    results = exchange(
        (
            hidden_rows, expert_ids.transpose(1, 2, 0), route_weights.transpose(1, 2, 0), codes,
            owner_slot.reshape(1, -1), conv_state.transpose(1, 0, 2), conv_taps, conv_bias.reshape(1, -1), upsample,
        ),
        w_gate, w_up, w_down.reshape(-1, width), code_table.reshape(books * shard, channels),
        experts, books,
    )
    vm_spec = pl.BlockSpec(memory_space=pltpu.VMEM)
    moe, samples, carried = pl.pallas_call(
        hand_over,
        out_shape=tuple(jax.ShapeDtypeStruct(r.shape, r.dtype) for r in results),
        in_specs=[vm_spec] * 3,
        out_specs=(vm_spec,) * 3,
    )(*results)
    return moe, samples, carried.transpose(1, 0, 2)


def solution(mesh):
    rows = P(("groups", "expert", "wave"), None, None)
    placed = (
        rows, rows, rows,
        P("expert", None, "wave"), P("expert", None, "wave"), P("expert", "wave", None),
        rows, P(("groups", "expert", "wave")), P(None, "expert", None), rows, P(), P(), P(),
    )
    return jax.shard_map(
        per_device, mesh=mesh, in_specs=placed, out_specs=(rows, rows, rows), check_vma=False
    )
```

```python
import functools

import jax
import jax.numpy as jnp
from jax import lax
from jax.experimental import pallas as pl
from jax.experimental.pallas import tpu as pltpu
from jax.sharding import PartitionSpec as P

MESH = pl.DeviceIdType.MESH
BF = jnp.bfloat16
F32 = jnp.float32
RADIX = 64
LANES = 128
INNER = 2
HALVES = 2


def dot(a, b):
    return jnp.dot(a, b, preferred_element_type=F32)


def kernel(
    n_e, experts, books,
    h_ref, id_ref, rw_ref, co_ref, ow_ref, st_ref, tap_ref, bias_ref, us_ref,
    wg_ref, wu_ref, wd_ref, tab_ref,
    moe_ref, wave_ref, new_ref,
    hv, idv, rwv, cov, owv, stv, tapv, biasv, usv,
    xg, meta, wgu, wdv, tabv, mem, act, early, told, po, pn, my, ma, mz, mine,
    fs, fy, fa, fz, fr,
    in_sem, w_sem, pws, pwr, zus, zds, yss, agr, mes, mer,
    mys, myr, mzs, mzr, fys, fyr, fzs, fzr, below, above, aside,
):
    outer = n_e // INNER
    sessions, steps, width = hv.shape
    rows = sessions * steps
    channels = tab_ref.shape[1]
    local, _, units = wg_ref.shape
    ff = 2 * units
    shard = tab_ref.shape[0] // books
    wave_rows = n_e * rows
    col_rows = outer * rows
    e = lax.axis_index("expert")
    w = lax.axis_index("wave")
    z = e // INNER
    y = e % INNER
    peer = 1 - w
    ye = z * INNER + (1 - y)
    low = z < outer // 2

    def remote(src, dst, ssem, rsem, te, tw):
        return pltpu.make_async_remote_copy(
            src_ref=src, dst_ref=dst, send_sem=ssem, recv_sem=rsem,
            device_id={"expert": te, "wave": tw}, device_id_type=MESH,
        )

    barrier = pltpu.get_barrier_semaphore()

    def greet(te, tw):
        pl.semaphore_signal(barrier, inc=1, device_id={"expert": te, "wave": tw}, device_id_type=MESH)

    greet(e, peer)
    greet(ye, w)

    @pl.when(z > 0)
    def _():
        greet(e - INNER, w)

    @pl.when(z < outer - 1)
    def _():
        greet(e + INNER, w)

    firsts = [
        pltpu.make_async_copy(src, dst, in_sem.at[i])
        for i, (src, dst) in enumerate((
            (h_ref, hv), (id_ref, idv), (rw_ref, rwv), (co_ref, cov), (ow_ref, owv),
            (st_ref, stv), (tap_ref, tapv), (bias_ref, biasv), (us_ref, usv),
        ))
    ]
    for copy in firsts[:5]:
        copy.start()

    def gate_at(tw):
        return pl.ds(pl.multiple_of(tw * units, LANES), units)

    def up_at(tw):
        return pl.ds(pl.multiple_of(ff + tw * units, LANES), units)

    def down_at(j, tw):
        return pl.ds(pl.multiple_of(j * ff + tw * units, LANES), units)

    def weights(tw):
        pairs = []
        for j in range(local):
            pairs.append((wg_ref.at[j], wgu.at[j, :, gate_at(tw)]))
            pairs.append((wu_ref.at[j], wgu.at[j, :, up_at(tw)]))
        for j in range(local):
            pairs.append((wd_ref.at[pl.ds(j * units, units), :], wdv.at[down_at(j, tw), :]))
        return pairs

    loads = [
        pltpu.make_async_copy(src, dst, w_sem.at[i]) for i, (src, dst) in enumerate(weights(w))
    ]
    table = pltpu.make_async_copy(tab_ref, tabv, w_sem.at[3 * local])
    gives = [
        remote(src, dst, pws.at[i], pwr.at[i], e, peer) for i, (src, dst) in enumerate(weights(w))
    ]
    takes = [
        remote(src, dst, pws.at[i], pwr.at[i], e, peer) for i, (src, dst) in enumerate(weights(peer))
    ]

    half = rows // HALVES

    def at(rel, zo, p):
        return pl.ds(pl.multiple_of((rel * outer + zo) * rows + p * half, half), half)

    def agsem(rel, zo, p):
        return agr.at[(rel * outer + zo) * HALVES + p]

    def up(zo, p):
        s = xg.at[at(0, zo, p), :]
        return remote(s, s, zus.at[zo * HALVES + p], agsem(0, zo, p), (z + 1) * INNER + y, w)

    def down(zo, p):
        s = xg.at[at(0, zo, p), :]
        return remote(s, s, zds.at[zo * HALVES + p], agsem(0, zo, p), (z - 1) * INNER + y, w)

    def across(zo, p):
        return remote(
            xg.at[at(0, zo, p), :], xg.at[at(1, zo, p), :], yss.at[zo * HALVES + p], agsem(1, zo, p), ye, w
        )

    def arrived(rel, zo, p):
        s = xg.at[at(rel, zo, p), :]
        remote(s, s, yss.at[0], agsem(rel, zo, p), ye, w).wait_recv()

    def meta_at(te, se):
        rel = (te % INNER + se % INNER) % 2
        return pl.ds(pl.multiple_of((rel * outer + se // INNER) * rows, rows), rows)

    def tell(d):
        te = (e + d) % n_e
        return remote(
            meta.at[meta_at(e, e), :], meta.at[meta_at(te, e), :], mes.at[d - 1], mer.at[d - 1], te, w
        )

    def told_by(d):
        se = (e - d + n_e) % n_e
        s = meta.at[meta_at(e, se), :]
        return remote(s, s, mes.at[d - 1], mer.at[d - 1], se, w)

    firsts[0].wait()
    hid = hv[...]
    mine_at = pl.multiple_of(z * rows, rows)
    for t in range(steps):
        xg[pl.ds(mine_at + t * sessions, sessions), :] = hid[:, t, :]
    for copy in firsts[5:]:
        copy.start()
    table.start()
    for load in loads:
        load.start()
    pl.semaphore_wait(barrier, 2 + (z > 0).astype(jnp.int32) + (z < outer - 1).astype(jnp.int32))

    for p in range(HALVES):
        @pl.when(z + 1 < outer)
        def _():
            up(z, p).start()

        @pl.when(z > 0)
        def _():
            down(z, p).start()

        across(z, p).start()
    for give in gives:
        give.start()

    lanes = meta.shape[1]
    dest_at = 2 * experts
    code_at = dest_at + 8

    def placed(count, start):
        here = lax.broadcasted_iota(jnp.int32, (count, lanes), 0)
        there = lax.broadcasted_iota(jnp.int32, (count, lanes), 1)
        return jnp.where(here + start == there, 1.0, 0.0).astype(BF)

    for copy in firsts[1:5]:
        copy.wait()
    owner = owv[...].astype(F32)
    holder = jnp.floor((owner + 0.5) / sessions)
    within = owner - holder * sessions
    holder = jnp.floor((holder + 0.5) / 2)
    expert_i = lax.broadcasted_iota(jnp.int32, (experts, sessions), 0)
    digit = lax.broadcasted_iota(jnp.int32, (8, sessions), 0)
    for t in range(steps):
        both = jnp.zeros((experts, sessions), F32)
        for k in range(idv.shape[1]):
            both += jnp.where(expert_i == idv[t, k:k + 1, :], rwv[t, k:k + 1, :], 0.0)
        high = both.astype(BF).astype(F32)
        dest = holder * rows + t * sessions + within
        top = jnp.floor((dest + 0.5) / RADIX)
        digits = jnp.where(digit == 0, top, jnp.where(digit == 1, dest - top * RADIX, 0.0))
        upright = jnp.concatenate([high, both - high, digits], axis=0).astype(BF)
        extra = lax.dot_general(
            upright, placed(code_at, 0), (((0,), (0,)), ((), ())), preferred_element_type=F32
        )
        co = cov[:, t, :].astype(F32)
        top = jnp.floor((co + 0.5) / RADIX)
        extra += dot(top.astype(BF), placed(books, code_at))
        extra += dot((co - top * RADIX).astype(BF), placed(books, code_at + books))
        meta[pl.ds(mine_at + t * sessions, sessions), :] = extra.astype(BF)

    def signal(sem, te):
        pl.semaphore_signal(sem, inc=1, device_id={"expert": te, "wave": w}, device_id_type=MESH)

    def upward():
        @pl.when(z > 0)
        def _():
            pl.semaphore_wait(below, 1)

        @pl.when(z < outer - 1)
        def _():
            signal(below, e + INNER)

    def downward():
        @pl.when(z < outer - 1)
        def _():
            pl.semaphore_wait(above, 1)

        @pl.when(z > 0)
        def _():
            signal(above, e - INNER)

    @pl.when(low)
    def _():
        upward()
        downward()

    @pl.when(jnp.logical_not(low))
    def _():
        downward()
        upward()

    signal(aside, ye)
    pl.semaphore_wait(aside, 1)
    for d in range(1, n_e):
        tell(d).start()

    for copy in firsts[5:]:
        copy.wait()
    state_len = stv.shape[0]
    taps = tapv.shape[0]

    def before():
        for t in range(steps):
            total = jnp.broadcast_to(biasv[...], (sessions, channels))
            for j in range(t + 1, taps):
                total += tapv[j:j + 1, :] * stv[state_len + t - j].astype(F32)
            early[t * sessions:(t + 1) * sessions, :] = total
        for i in range(state_len - steps):
            new_ref[i] = stv[i + steps]

    def forward(step):
        for p in range(HALVES):
            @pl.when(z - step >= 0)
            def _():
                zo = z - step
                arrived(0, zo, p)

                @pl.when(z + 1 < outer)
                def _():
                    up(zo, p).start()

                across(zo, p).start()

            @pl.when(z + step < outer)
            def _():
                zo = z + step
                arrived(0, zo, p)

                @pl.when(z > 0)
                def _():
                    down(zo, p).start()

                across(zo, p).start()

    src = lax.broadcasted_iota(jnp.int32, (lanes, LANES), 0)
    col = lax.broadcasted_iota(jnp.int32, (lanes, LANES), 1)

    def learn():
        for d in range(1, n_e):
            told_by(d).wait_recv()
        is_code = col < books
        pick = jnp.where(is_code & (src == code_at + col), float(RADIX), 0.0)
        pick += jnp.where(is_code & (src == code_at + books + col), 1.0, 0.0)
        pick += jnp.where((col == books) & (src == dest_at), float(RADIX), 0.0)
        pick += jnp.where((col == books) & (src == dest_at + 1), 1.0, 0.0)
        own = e * local + col - (books + 1)
        is_weight = (col > books) & (col <= books + local)
        pick += jnp.where(is_weight & ((src == own) | (src == own + experts)), 1.0, 0.0)
        told[...] = dot(meta[...], pick.astype(BF))
        lane = lax.broadcasted_iota(jnp.int32, (wave_rows, shard), 1).astype(F32)
        first = (e * shard).astype(F32)
        for q in range(books):
            mem[:, q * shard:(q + 1) * shard] = jnp.where(
                told[:, q:q + 1] - first == lane, 1.0, 0.0
            ).astype(BF)

    def embed():
        place = lax.broadcasted_iota(jnp.int32, (wave_rows, wave_rows), 1).astype(F32)
        order = jnp.where(told[:, books:books + 1] == place, 1.0, 0.0).astype(BF)
        table.wait()
        f_tile = min(channels, 512)

        @pl.loop(0, channels // f_tile)
        def _(n):
            cols = pl.ds(pl.multiple_of(n * f_tile, f_tile), f_tile)
            part = dot(mem[...], tabv[:, cols]).astype(BF)
            fs[:, cols] = lax.dot_general(
                order, part, (((0,), (0,)), ((), ())), preferred_element_type=F32
            ).astype(BF)

    def goal(k):
        if k == outer - 1:
            return z
        down_from = outer - 1 - k
        down_from = down_from - (down_from <= z).astype(jnp.int32)
        up_from = k + (k >= z).astype(jnp.int32)
        return jnp.where(low, down_from, up_from)

    def block(zo, yo):
        return pl.ds(pl.multiple_of((zo * INNER + yo) * rows, rows), rows)

    def zrows(zo):
        return pl.ds(pl.multiple_of(zo * rows, rows), rows)

    def hop(zo):
        return (zo - z + outer) % outer - 1

    def fy_copy(zo):
        return remote(fs.at[block(zo, 1 - y), :], fy.at[zrows(zo), :], fys.at[zo], fyr.at[zo], ye, w)

    def fz_copy(zo):
        d = hop(zo)
        return remote(fa.at[zrows(zo), :], fz.at[zrows(d), :], fzs.at[d], fzr.at[d], zo * INNER + y, w)

    def fz_got(d):
        s = fz.at[zrows(d), :]
        return remote(s, s, fzs.at[d], fzr.at[d], ye, w)

    part_cols = width // HALVES

    def cols_of(p):
        return pl.ds(p * part_cols, part_cols)

    def my_copy(zo, p):
        i = zo * HALVES + p
        return remote(
            pn.at[zrows(zo), cols_of(p)], my.at[zrows(zo), cols_of(p)], mys.at[i], myr.at[i], ye, w
        )

    def mz_copy(zo, p):
        there = (z - zo + outer) % outer
        return remote(
            ma.at[zrows(zo), cols_of(p)], mz.at[zrows(there), cols_of(p)],
            mzs.at[zo * HALVES + p], mzr.at[there * HALVES + p], zo * INNER + y, w,
        )

    def mz_got(there, p):
        s = mz.at[zrows(there), cols_of(p)]
        return remote(s, s, mzs.at[0], mzr.at[there * HALVES + p], ye, w)

    rc = min(col_rows, 128)

    def looped(count, body):
        if count == 1:
            body(0)
        else:
            pl.loop(0, count)(body)

    def ready(i):
        loads[i].wait()
        takes[i].wait_recv()

    def hidden(rel, j):
        def piece(i):
            here = pl.ds(pl.multiple_of(rel * col_rows + i * rc, rc), rc)
            x = xg[here, :]
            weight = told[here, books + 1 + j:books + 2 + j]
            tile = ff // 3 if ff % (3 * LANES) == 0 else ff
            for n in range(0, ff, tile):
                g = dot(x, wgu[j, :, n:n + tile])
                u = dot(x, wgu[j, :, ff + n:ff + n + tile])
                a = g / (1.0 + jnp.exp(-g)) * u * weight
                act[here, j * ff + n:j * ff + n + tile] = a.astype(BF)

        looped(col_rows // rc, piece)

    def project(rel, dst, p):
        def piece(i):
            here = pl.ds(pl.multiple_of(rel * col_rows + i * rc, rc), rc)
            there = pl.ds(pl.multiple_of(i * rc, rc), rc)
            tile = min(part_cols, 512)
            for n in range(p * part_cols, (p + 1) * part_cols, tile):
                dst[there, n:n + tile] = dot(act[here, :], wdv[:, n:n + tile]).astype(BF)

        looped(col_rows // rc, piece)

    def frames_on(k):
        zo = goal(k)
        total = fs[block(zo, y), :].astype(F32)
        fy_copy(zo).wait_recv()
        total += fy[zrows(zo), :].astype(F32)
        if k < outer - 1:
            fa[zrows(zo), :] = total.astype(BF)
            fz_copy(zo).start()
        else:
            fr[...] = total

    before()
    for step in range(1, outer):
        forward(step)
        if step == 1:
            learn()
        if step == min(2, outer - 1):
            embed()
    for k in range(outer):
        fy_copy(goal(k)).start()

    for j in range(local):
        ready(2 * j)
        ready(2 * j + 1)
        hidden(0, j)
    for zo in range(outer):
        for p in range(HALVES):
            arrived(1, zo, p)
    for j in range(local):
        hidden(1, j)
        if j < outer - 1:
            frames_on(j)
    for j in range(local):
        ready(2 * local + j)
    for p in range(HALVES):
        project(1, pn, p)
        my_copy(goal(0), p).start()
    for k in range(1, outer):
        for p in range(HALVES):
            my_copy(goal(k), p).start()
    for k in range(min(local, outer - 1), outer):
        frames_on(k)
    for p in range(HALVES):
        project(0, po, p)

    def pass_on(k):
        zo = goal(k)
        for p in range(HALVES):
            my_copy(zo, p).wait_recv()
            here = (zrows(zo), cols_of(p))
            ma[here] = (po[here].astype(F32) + my[here].astype(F32)).astype(BF)
            mz_copy(zo, p).start()

    def finish_frames():
        for d in range(outer - 1):
            fz_got(d).wait_recv()
            fr[...] += fz[zrows(d), :].astype(F32)
        got = [fr[t * sessions:(t + 1) * sessions, :] for t in range(steps)]
        decoded = []
        for t in range(steps):
            total = early[t * sessions:(t + 1) * sessions, :]
            for j in range(t + 1):
                total += tapv[j:j + 1, :] * got[t - j]
            decoded.append(jax.nn.gelu(total).astype(BF))
            new_ref[state_len - steps + t] = got[t].astype(BF)
        samples = dot(jnp.concatenate(decoded, axis=0), usv[...]).astype(BF)
        for t in range(steps):
            wave_ref[:, t, :] = samples[t * sessions:(t + 1) * sessions]

    for k in range(outer - 1):
        pass_on(k)
    finish_frames()
    for p in range(HALVES):
        my_copy(z, p).wait_recv()
        mine[...] = po[zrows(z), cols_of(p)].astype(F32) + my[zrows(z), cols_of(p)].astype(F32)

        for d in range(1, outer):
            mz_got(d, p).wait_recv()
            mine[...] += mz[zrows(d), cols_of(p)].astype(F32)

        for t in range(steps):
            moe_ref[:, t, p * part_cols:(p + 1) * part_cols] = mine[t * sessions:(t + 1) * sessions, :].astype(BF)

    for give in gives:
        give.wait_send()
    for d in range(1, n_e):
        tell(d).wait_send()
    for zo in range(outer):
        for p in range(HALVES):
            @pl.when((z + 1 < outer) & (zo <= z))
            def _():
                up(zo, p).wait_send()

            @pl.when((z > 0) & (zo >= z))
            def _():
                down(zo, p).wait_send()

            across(zo, p).wait_send()
            my_copy(zo, p).wait_send()
        fy_copy(zo).wait_send()
    for k in range(outer - 1):
        zo = goal(k)
        fz_copy(zo).wait_send()
        for p in range(HALVES):
            mz_copy(zo, p).wait_send()


def hand_over(a_ref, b_ref, c_ref, a_out, b_out, c_out):
    a_out[...] = a_ref[...]
    b_out[...] = b_ref[...]
    c_out[...] = c_ref[...]


def exchange(args, w_gate, w_up, w_down, table, experts, books):
    n_e = lax.axis_size("expert")
    outer = n_e // INNER
    sessions, steps, width = args[0].shape
    rows = sessions * steps
    used = 2 * experts + 8 + 2 * books
    lanes = used + -used % LANES
    local, _, units = w_gate.shape
    ff = 2 * units
    channels = table.shape[1]
    wave_rows = n_e * rows
    col_rows = outer * rows
    vm = pltpu.VMEM
    dma = lambda *s: pltpu.SemaphoreType.DMA(s)
    hops = outer - 1
    scratch = [vm(a.shape, a.dtype) for a in args] + [
        vm((wave_rows, width), BF),
        vm((wave_rows, lanes), BF),
        vm((local, width, 2 * ff), BF),
        vm((local * ff, width), BF),
        vm(table.shape, BF),
        vm((wave_rows, table.shape[0]), BF),
        vm((wave_rows, local * ff), BF),
        vm((rows, channels), F32),
        vm((wave_rows, LANES), F32),
        vm((col_rows, width), BF),
        vm((col_rows, width), BF),
        vm((col_rows, width), BF),
        vm((col_rows, width), BF),
        vm((outer * rows, width), BF),
        vm((rows, width // HALVES), F32),
        vm((wave_rows, channels), BF),
        vm((col_rows, channels), BF),
        vm((col_rows, channels), BF),
        vm((hops * rows, channels), BF),
        vm((rows, channels), F32),
        dma(len(args)), dma(3 * local + 1), dma(3 * local), dma(3 * local),
        dma(outer * HALVES), dma(outer * HALVES), dma(outer * HALVES), dma(n_e * HALVES),
        dma(n_e - 1), dma(n_e - 1),
        dma(outer * HALVES), dma(outer * HALVES), dma(outer * HALVES), dma(outer * HALVES),
        dma(outer), dma(outer), dma(hops), dma(hops),
        pltpu.SemaphoreType.REGULAR, pltpu.SemaphoreType.REGULAR, pltpu.SemaphoreType.REGULAR,
    ]
    any_spec = pl.BlockSpec(memory_space=pl.ANY)
    vm_spec = pl.BlockSpec(memory_space=pltpu.VMEM)
    return pl.pallas_call(
        functools.partial(kernel, n_e, experts, books),
        out_shape=(
            jax.ShapeDtypeStruct((sessions, steps, width), BF),
            jax.ShapeDtypeStruct((sessions, steps, args[8].shape[1]), BF),
            jax.ShapeDtypeStruct(args[5].shape, BF),
        ),
        in_specs=[any_spec] * (len(args) + 4),
        out_specs=(vm_spec, vm_spec, vm_spec),
        scratch_shapes=scratch,
        compiler_params=pltpu.CompilerParams(
            collective_id=0, has_side_effects=True, vmem_limit_bytes=60 * 1024 * 1024
        ),
    )(*args, w_gate, w_up, w_down, table)


def per_device(
    hidden_rows, expert_ids, route_weights, w_gate, w_up, w_down,
    codes, owner_slot, code_table, conv_state, conv_taps, conv_bias, upsample,
):
    n_e = lax.axis_size("expert")
    width = hidden_rows.shape[2]
    experts = n_e * w_gate.shape[0]
    books, shard, channels = code_table.shape
    results = exchange(
        (
            hidden_rows, expert_ids.transpose(1, 2, 0), route_weights.transpose(1, 2, 0), codes,
            owner_slot.reshape(1, -1), conv_state.transpose(1, 0, 2), conv_taps, conv_bias.reshape(1, -1), upsample,
        ),
        w_gate, w_up, w_down.reshape(-1, width), code_table.reshape(books * shard, channels),
        experts, books,
    )
    vm_spec = pl.BlockSpec(memory_space=pltpu.VMEM)
    moe, samples, carried = pl.pallas_call(
        hand_over,
        out_shape=tuple(jax.ShapeDtypeStruct(r.shape, r.dtype) for r in results),
        in_specs=[vm_spec] * 3,
        out_specs=(vm_spec,) * 3,
    )(*results)
    return moe, samples, carried.transpose(1, 0, 2)


def solution(mesh):
    rows = P(("groups", "expert", "wave"), None, None)
    placed = (
        rows, rows, rows,
        P("expert", None, "wave"), P("expert", None, "wave"), P("expert", "wave", None),
        rows, P(("groups", "expert", "wave")), P(None, "expert", None), rows, P(), P(), P(),
    )
    return jax.shard_map(
        per_device, mesh=mesh, in_specs=placed, out_specs=(rows, rows, rows), check_vma=False
    )
```

```python
import functools

import jax
import jax.numpy as jnp
from jax import lax
from jax.experimental import pallas as pl
from jax.experimental.pallas import tpu as pltpu
from jax.sharding import PartitionSpec as P

MESH = pl.DeviceIdType.MESH
BF = jnp.bfloat16
F32 = jnp.float32
RADIX = 64
LANES = 128
INNER = 2
HALVES = 2


def dot(a, b):
    return jnp.dot(a, b, preferred_element_type=F32)


def kernel(
    n_e, experts, books,
    h_ref, id_ref, rw_ref, co_ref, ow_ref, st_ref, tap_ref, bias_ref, us_ref,
    wg_ref, wu_ref, wd_ref, tab_ref,
    moe_ref, wave_ref, new_ref,
    hv, idv, rwv, cov, owv, stv, tapv, biasv, usv,
    xg, meta, wgu, wdv, tabv, mem, act, early, told, po, pn, my, ma, mz, mine,
    fs, fy, fa, fz, gz, ga, gy, fr,
    in_sem, w_sem, pws, pwr, zus, zds, yss, agr, mes, mer,
    mys, myr, mzs, mzr, fys, fyr, fzs, fzr, gzs, gzr, gys, below, above, aside,
):
    outer = n_e // INNER
    sessions, steps, width = hv.shape
    rows = sessions * steps
    channels = tab_ref.shape[1]
    local, _, units = wg_ref.shape
    ff = 2 * units
    shard = tab_ref.shape[0] // books
    wave_rows = n_e * rows
    col_rows = outer * rows
    e = lax.axis_index("expert")
    w = lax.axis_index("wave")
    z = e // INNER
    y = e % INNER
    peer = 1 - w
    ye = z * INNER + (1 - y)
    low = z < outer // 2

    def remote(src, dst, ssem, rsem, te, tw):
        return pltpu.make_async_remote_copy(
            src_ref=src, dst_ref=dst, send_sem=ssem, recv_sem=rsem,
            device_id={"expert": te, "wave": tw}, device_id_type=MESH,
        )

    barrier = pltpu.get_barrier_semaphore()

    def greet(te, tw):
        pl.semaphore_signal(barrier, inc=1, device_id={"expert": te, "wave": tw}, device_id_type=MESH)

    greet(e, peer)
    greet(ye, w)

    @pl.when(z > 0)
    def _():
        greet(e - INNER, w)

    @pl.when(z < outer - 1)
    def _():
        greet(e + INNER, w)

    firsts = [
        pltpu.make_async_copy(src, dst, in_sem.at[i])
        for i, (src, dst) in enumerate((
            (h_ref, hv), (id_ref, idv), (rw_ref, rwv), (co_ref, cov), (ow_ref, owv),
            (st_ref, stv), (tap_ref, tapv), (bias_ref, biasv), (us_ref, usv),
        ))
    ]
    for copy in firsts[:5]:
        copy.start()

    def gate_at(tw):
        return pl.ds(pl.multiple_of(tw * units, LANES), units)

    def up_at(tw):
        return pl.ds(pl.multiple_of(ff + tw * units, LANES), units)

    def down_at(j, tw):
        return pl.ds(pl.multiple_of(j * ff + tw * units, LANES), units)

    def weights(tw):
        pairs = []
        for j in range(local):
            pairs.append((wg_ref.at[j], wgu.at[j, :, gate_at(tw)]))
            pairs.append((wu_ref.at[j], wgu.at[j, :, up_at(tw)]))
        for j in range(local):
            pairs.append((wd_ref.at[pl.ds(j * units, units), :], wdv.at[down_at(j, tw), :]))
        return pairs

    loads = [
        pltpu.make_async_copy(src, dst, w_sem.at[i]) for i, (src, dst) in enumerate(weights(w))
    ]
    table = pltpu.make_async_copy(tab_ref, tabv, w_sem.at[3 * local])
    gives = [
        remote(src, dst, pws.at[i], pwr.at[i], e, peer) for i, (src, dst) in enumerate(weights(w))
    ]
    takes = [
        remote(src, dst, pws.at[i], pwr.at[i], e, peer) for i, (src, dst) in enumerate(weights(peer))
    ]

    half = rows // HALVES

    def at(rel, zo, p):
        return pl.ds(pl.multiple_of((rel * outer + zo) * rows + p * half, half), half)

    def agsem(rel, zo, p):
        return agr.at[(rel * outer + zo) * HALVES + p]

    def up(zo, p):
        s = xg.at[at(0, zo, p), :]
        return remote(s, s, zus.at[zo * HALVES + p], agsem(0, zo, p), (z + 1) * INNER + y, w)

    def down(zo, p):
        s = xg.at[at(0, zo, p), :]
        return remote(s, s, zds.at[zo * HALVES + p], agsem(0, zo, p), (z - 1) * INNER + y, w)

    def across(zo, p):
        return remote(
            xg.at[at(0, zo, p), :], xg.at[at(1, zo, p), :], yss.at[zo * HALVES + p], agsem(1, zo, p), ye, w
        )

    def arrived(rel, zo, p):
        s = xg.at[at(rel, zo, p), :]
        remote(s, s, yss.at[0], agsem(rel, zo, p), ye, w).wait_recv()

    def meta_at(te, se):
        rel = (te % INNER + se % INNER) % 2
        return pl.ds(pl.multiple_of((rel * outer + se // INNER) * rows, rows), rows)

    def tell(d):
        te = (e + d) % n_e
        return remote(
            meta.at[meta_at(e, e), :], meta.at[meta_at(te, e), :], mes.at[d - 1], mer.at[d - 1], te, w
        )

    def told_by(d):
        se = (e - d + n_e) % n_e
        s = meta.at[meta_at(e, se), :]
        return remote(s, s, mes.at[d - 1], mer.at[d - 1], se, w)

    firsts[0].wait()
    hid = hv[...]
    mine_at = pl.multiple_of(z * rows, rows)
    for t in range(steps):
        xg[pl.ds(mine_at + t * sessions, sessions), :] = hid[:, t, :]
    for copy in firsts[5:]:
        copy.start()
    table.start()
    for load in loads:
        load.start()
    pl.semaphore_wait(barrier, 2 + (z > 0).astype(jnp.int32) + (z < outer - 1).astype(jnp.int32))

    for p in range(HALVES):
        @pl.when(z + 1 < outer)
        def _():
            up(z, p).start()

        @pl.when(z > 0)
        def _():
            down(z, p).start()

        across(z, p).start()
    for give in gives:
        give.start()

    lanes = meta.shape[1]
    dest_at = 2 * experts
    code_at = dest_at + 8

    def placed(count, start):
        here = lax.broadcasted_iota(jnp.int32, (count, lanes), 0)
        there = lax.broadcasted_iota(jnp.int32, (count, lanes), 1)
        return jnp.where(here + start == there, 1.0, 0.0).astype(BF)

    for copy in firsts[1:5]:
        copy.wait()
    owner = owv[...].astype(F32)
    holder = jnp.floor((owner + 0.5) / sessions)
    within = owner - holder * sessions
    holder = jnp.floor((holder + 0.5) / 2)
    expert_i = lax.broadcasted_iota(jnp.int32, (experts, sessions), 0)
    digit = lax.broadcasted_iota(jnp.int32, (8, sessions), 0)
    for t in range(steps):
        both = jnp.zeros((experts, sessions), F32)
        for k in range(idv.shape[1]):
            both += jnp.where(expert_i == idv[t, k:k + 1, :], rwv[t, k:k + 1, :], 0.0)
        high = both.astype(BF).astype(F32)
        dest = holder * rows + t * sessions + within
        top = jnp.floor((dest + 0.5) / RADIX)
        digits = jnp.where(digit == 0, top, jnp.where(digit == 1, dest - top * RADIX, 0.0))
        upright = jnp.concatenate([high, both - high, digits], axis=0).astype(BF)
        extra = lax.dot_general(
            upright, placed(code_at, 0), (((0,), (0,)), ((), ())), preferred_element_type=F32
        )
        co = cov[:, t, :].astype(F32)
        top = jnp.floor((co + 0.5) / RADIX)
        extra += dot(top.astype(BF), placed(books, code_at))
        extra += dot((co - top * RADIX).astype(BF), placed(books, code_at + books))
        meta[pl.ds(mine_at + t * sessions, sessions), :] = extra.astype(BF)

    def signal(sem, te):
        pl.semaphore_signal(sem, inc=1, device_id={"expert": te, "wave": w}, device_id_type=MESH)

    def upward():
        @pl.when(z > 0)
        def _():
            pl.semaphore_wait(below, 1)

        @pl.when(z < outer - 1)
        def _():
            signal(below, e + INNER)

    def downward():
        @pl.when(z < outer - 1)
        def _():
            pl.semaphore_wait(above, 1)

        @pl.when(z > 0)
        def _():
            signal(above, e - INNER)

    @pl.when(low)
    def _():
        upward()
        downward()

    @pl.when(jnp.logical_not(low))
    def _():
        downward()
        upward()

    signal(aside, ye)
    pl.semaphore_wait(aside, 1)
    for d in range(1, n_e):
        tell(d).start()

    for copy in firsts[5:]:
        copy.wait()
    state_len = stv.shape[0]
    taps = tapv.shape[0]

    def before():
        for t in range(steps):
            total = jnp.broadcast_to(biasv[...], (sessions, channels))
            for j in range(t + 1, taps):
                total += tapv[j:j + 1, :] * stv[state_len + t - j].astype(F32)
            early[t * sessions:(t + 1) * sessions, :] = total
        for i in range(state_len - steps):
            new_ref[i] = stv[i + steps]

    def forward(step):
        for p in range(HALVES):
            @pl.when(z - step >= 0)
            def _():
                zo = z - step
                arrived(0, zo, p)

                @pl.when(z + 1 < outer)
                def _():
                    up(zo, p).start()

                across(zo, p).start()

            @pl.when(z + step < outer)
            def _():
                zo = z + step
                arrived(0, zo, p)

                @pl.when(z > 0)
                def _():
                    down(zo, p).start()

                across(zo, p).start()

    src = lax.broadcasted_iota(jnp.int32, (lanes, LANES), 0)
    col = lax.broadcasted_iota(jnp.int32, (lanes, LANES), 1)

    def learn():
        for d in range(1, n_e):
            told_by(d).wait_recv()
        is_code = col < books
        pick = jnp.where(is_code & (src == code_at + col), float(RADIX), 0.0)
        pick += jnp.where(is_code & (src == code_at + books + col), 1.0, 0.0)
        pick += jnp.where((col == books) & (src == dest_at), float(RADIX), 0.0)
        pick += jnp.where((col == books) & (src == dest_at + 1), 1.0, 0.0)
        own = e * local + col - (books + 1)
        is_weight = (col > books) & (col <= books + local)
        pick += jnp.where(is_weight & ((src == own) | (src == own + experts)), 1.0, 0.0)
        told[...] = dot(meta[...], pick.astype(BF))
        lane = lax.broadcasted_iota(jnp.int32, (wave_rows, shard), 1).astype(F32)
        first = (e * shard).astype(F32)
        for q in range(books):
            mem[:, q * shard:(q + 1) * shard] = jnp.where(
                told[:, q:q + 1] - first == lane, 1.0, 0.0
            ).astype(BF)

    def embed():
        place = lax.broadcasted_iota(jnp.int32, (wave_rows, wave_rows), 1).astype(F32)
        order = jnp.where(told[:, books:books + 1] == place, 1.0, 0.0).astype(BF)
        table.wait()
        f_tile = min(channels, 512)

        @pl.loop(0, channels // f_tile)
        def _(n):
            cols = pl.ds(pl.multiple_of(n * f_tile, f_tile), f_tile)
            part = dot(mem[...], tabv[:, cols]).astype(BF)
            fs[:, cols] = lax.dot_general(
                order, part, (((0,), (0,)), ((), ())), preferred_element_type=F32
            ).astype(BF)

    def goal(k):
        if k == outer - 1:
            return z
        down_from = outer - 1 - k
        down_from = down_from - (down_from <= z).astype(jnp.int32)
        up_from = k + (k >= z).astype(jnp.int32)
        return jnp.where(low, down_from, up_from)

    def block(zo, yo):
        return pl.ds(pl.multiple_of((zo * INNER + yo) * rows, rows), rows)

    def zrows(zo):
        return pl.ds(pl.multiple_of(zo * rows, rows), rows)

    def hop(zo):
        return (zo - z + outer) % outer - 1

    split = channels // 2
    first_half = pl.ds(0, split)
    second_half = pl.ds(split, split)

    def pair(zo):
        return pl.ds(pl.multiple_of(zo * INNER * rows, INNER * rows), INNER * rows)

    def fy_copy(zo):
        return remote(fs.at[block(zo, 1 - y), first_half], fy.at[zrows(zo), :], fys.at[zo], fyr.at[zo], ye, w)

    def fz_copy(zo):
        d = hop(zo)
        return remote(fa.at[zrows(zo), :], fz.at[zrows(d), :], fzs.at[d], fzr.at[d], zo * INNER + y, w)

    def fz_got(d):
        s = fz.at[zrows(d), :]
        return remote(s, s, fzs.at[d], fzr.at[d], ye, w)

    def gz_copy(zo):
        d = hop(zo)
        return remote(fs.at[pair(zo), second_half], gz.at[pair(d), :], gzs.at[d], gzr.at[d], zo * INNER + y, w)

    def gz_got(d):
        s = gz.at[pair(d), :]
        return remote(s, s, gzs.at[d], gzr.at[d], ye, w)

    def gy_copy():
        return remote(ga, gy, gys.at[0], gys.at[1], ye, w)

    part_cols = width // HALVES

    def cols_of(p):
        return pl.ds(p * part_cols, part_cols)

    def my_copy(zo, p):
        i = zo * HALVES + p
        return remote(
            pn.at[zrows(zo), cols_of(p)], my.at[zrows(zo), cols_of(p)], mys.at[i], myr.at[i], ye, w
        )

    def mz_copy(zo, p):
        there = (z - zo + outer) % outer
        return remote(
            ma.at[zrows(zo), cols_of(p)], mz.at[zrows(there), cols_of(p)],
            mzs.at[zo * HALVES + p], mzr.at[there * HALVES + p], zo * INNER + y, w,
        )

    def mz_got(there, p):
        s = mz.at[zrows(there), cols_of(p)]
        return remote(s, s, mzs.at[0], mzr.at[there * HALVES + p], ye, w)

    rc = min(col_rows, 128)

    def looped(count, body):
        if count == 1:
            body(0)
        else:
            pl.loop(0, count)(body)

    def ready(i):
        loads[i].wait()
        takes[i].wait_recv()

    def hidden(rel, j):
        def piece(i):
            here = pl.ds(pl.multiple_of(rel * col_rows + i * rc, rc), rc)
            x = xg[here, :]
            weight = told[here, books + 1 + j:books + 2 + j]
            tile = ff // 3 if ff % (3 * LANES) == 0 else ff
            for n in range(0, ff, tile):
                g = dot(x, wgu[j, :, n:n + tile])
                u = dot(x, wgu[j, :, ff + n:ff + n + tile])
                a = g / (1.0 + jnp.exp(-g)) * u * weight
                act[here, j * ff + n:j * ff + n + tile] = a.astype(BF)

        looped(col_rows // rc, piece)

    def project(rel, dst, p):
        def piece(i):
            here = pl.ds(pl.multiple_of(rel * col_rows + i * rc, rc), rc)
            there = pl.ds(pl.multiple_of(i * rc, rc), rc)
            tile = min(part_cols, 512)
            for n in range(p * part_cols, (p + 1) * part_cols, tile):
                dst[there, n:n + tile] = dot(act[here, :], wdv[:, n:n + tile]).astype(BF)

        looped(col_rows // rc, piece)

    def frames_on(k):
        zo = goal(k)
        total = fs[block(zo, y), first_half].astype(F32)
        fy_copy(zo).wait_recv()
        total += fy[zrows(zo), :].astype(F32)
        if k < outer - 1:
            fa[zrows(zo), :] = total.astype(BF)
            fz_copy(zo).start()
        else:
            fr[:, first_half] = total

    before()
    for step in range(1, outer):
        forward(step)
        if step == 1:
            learn()
        if step == min(2, outer - 1):
            embed()
    for k in range(outer - 1):
        gz_copy(goal(k)).start()
    for k in range(outer):
        fy_copy(goal(k)).start()

    def both_ready(j):
        ready(2 * j)
        ready(2 * j + 1)

    both_ready(0)
    hidden(0, 0)
    for zo in range(outer):
        for p in range(HALVES):
            arrived(1, zo, p)
    for j in range(local):
        if j > 0:
            both_ready(j)
        hidden(1, j)
        if j < outer - 1:
            frames_on(j)
    for j in range(local):
        ready(2 * local + j)
    for p in range(HALVES):
        project(1, pn, p)
        my_copy(goal(0), p).start()
    for k in range(1, outer - 1):
        for p in range(HALVES):
            my_copy(goal(k), p).start()
    for k in range(min(local, outer - 1), outer):
        frames_on(k)
    for j in range(1, local):
        hidden(0, j)
    for p in range(HALVES):
        project(0, po, p)

    def frames_across():
        there = fs[block(z, 1 - y), second_half].astype(F32)
        here = fs[block(z, y), second_half].astype(F32)
        for d in range(outer - 1):
            gz_got(d).wait_recv()
            start = pl.multiple_of(d * INNER * rows, rows)
            there += gz[pl.ds(start + (1 - y) * rows, rows), :].astype(F32)
            here += gz[pl.ds(start + y * rows, rows), :].astype(F32)
        ga[...] = there.astype(BF)
        gy_copy().start()
        fr[:, second_half] = here

    def pass_on(k):
        zo = goal(k)
        for p in range(HALVES):
            my_copy(zo, p).wait_recv()
            here = (zrows(zo), cols_of(p))
            ma[here] = (po[here].astype(F32) + my[here].astype(F32)).astype(BF)
            mz_copy(zo, p).start()

    def finish_frames():
        for d in range(outer - 1):
            fz_got(d).wait_recv()
            fr[:, first_half] += fz[zrows(d), :].astype(F32)
        gy_copy().wait_recv()
        fr[:, second_half] += gy[...].astype(F32)
        got = [fr[t * sessions:(t + 1) * sessions, :] for t in range(steps)]
        decoded = []
        for t in range(steps):
            total = early[t * sessions:(t + 1) * sessions, :]
            for j in range(t + 1):
                total += tapv[j:j + 1, :] * got[t - j]
            decoded.append(jax.nn.gelu(total).astype(BF))
            new_ref[state_len - steps + t] = got[t].astype(BF)
        samples = dot(jnp.concatenate(decoded, axis=0), usv[...]).astype(BF)
        for t in range(steps):
            wave_ref[:, t, :] = samples[t * sessions:(t + 1) * sessions]

    pass_on(0)
    frames_across()
    for p in range(HALVES):
        my_copy(z, p).start()
    for k in range(1, outer - 1):
        pass_on(k)
    finish_frames()
    for p in range(HALVES):
        my_copy(z, p).wait_recv()
        mine[...] = po[zrows(z), cols_of(p)].astype(F32) + my[zrows(z), cols_of(p)].astype(F32)

        for d in range(1, outer):
            mz_got(d, p).wait_recv()
            mine[...] += mz[zrows(d), cols_of(p)].astype(F32)

        for t in range(steps):
            moe_ref[:, t, p * part_cols:(p + 1) * part_cols] = mine[t * sessions:(t + 1) * sessions, :].astype(BF)

    gy_copy().wait_send()
    for give in gives:
        give.wait_send()
    for d in range(1, n_e):
        tell(d).wait_send()
    for zo in range(outer):
        for p in range(HALVES):
            @pl.when((z + 1 < outer) & (zo <= z))
            def _():
                up(zo, p).wait_send()

            @pl.when((z > 0) & (zo >= z))
            def _():
                down(zo, p).wait_send()

            across(zo, p).wait_send()
            my_copy(zo, p).wait_send()
        fy_copy(zo).wait_send()
    for k in range(outer - 1):
        zo = goal(k)
        fz_copy(zo).wait_send()
        gz_copy(zo).wait_send()
        for p in range(HALVES):
            mz_copy(zo, p).wait_send()


def hand_over(a_ref, b_ref, c_ref, a_out, b_out, c_out):
    a_out[...] = a_ref[...]
    b_out[...] = b_ref[...]
    c_out[...] = c_ref[...]


def exchange(args, w_gate, w_up, w_down, table, experts, books):
    n_e = lax.axis_size("expert")
    outer = n_e // INNER
    sessions, steps, width = args[0].shape
    rows = sessions * steps
    used = 2 * experts + 8 + 2 * books
    lanes = used + -used % LANES
    local, _, units = w_gate.shape
    ff = 2 * units
    channels = table.shape[1]
    wave_rows = n_e * rows
    col_rows = outer * rows
    vm = pltpu.VMEM
    dma = lambda *s: pltpu.SemaphoreType.DMA(s)
    hops = outer - 1
    scratch = [vm(a.shape, a.dtype) for a in args] + [
        vm((wave_rows, width), BF),
        vm((wave_rows, lanes), BF),
        vm((local, width, 2 * ff), BF),
        vm((local * ff, width), BF),
        vm(table.shape, BF),
        vm((wave_rows, table.shape[0]), BF),
        vm((wave_rows, local * ff), BF),
        vm((rows, channels), F32),
        vm((wave_rows, LANES), F32),
        vm((col_rows, width), BF),
        vm((col_rows, width), BF),
        vm((col_rows, width), BF),
        vm((col_rows, width), BF),
        vm((outer * rows, width), BF),
        vm((rows, width // HALVES), F32),
        vm((wave_rows, channels), BF),
        vm((col_rows, channels // 2), BF),
        vm((col_rows, channels // 2), BF),
        vm((hops * rows, channels // 2), BF),
        vm((hops * INNER * rows, channels // 2), BF),
        vm((rows, channels // 2), BF),
        vm((rows, channels // 2), BF),
        vm((rows, channels), F32),
        dma(len(args)), dma(3 * local + 1), dma(3 * local), dma(3 * local),
        dma(outer * HALVES), dma(outer * HALVES), dma(outer * HALVES), dma(n_e * HALVES),
        dma(n_e - 1), dma(n_e - 1),
        dma(outer * HALVES), dma(outer * HALVES), dma(outer * HALVES), dma(outer * HALVES),
        dma(outer), dma(outer), dma(hops), dma(hops), dma(hops), dma(hops), dma(2),
        pltpu.SemaphoreType.REGULAR, pltpu.SemaphoreType.REGULAR, pltpu.SemaphoreType.REGULAR,
    ]
    any_spec = pl.BlockSpec(memory_space=pl.ANY)
    vm_spec = pl.BlockSpec(memory_space=pltpu.VMEM)
    return pl.pallas_call(
        functools.partial(kernel, n_e, experts, books),
        out_shape=(
            jax.ShapeDtypeStruct((sessions, steps, width), BF),
            jax.ShapeDtypeStruct((sessions, steps, args[8].shape[1]), BF),
            jax.ShapeDtypeStruct(args[5].shape, BF),
        ),
        in_specs=[any_spec] * (len(args) + 4),
        out_specs=(vm_spec, vm_spec, vm_spec),
        scratch_shapes=scratch,
        compiler_params=pltpu.CompilerParams(
            collective_id=0, has_side_effects=True, vmem_limit_bytes=60 * 1024 * 1024
        ),
    )(*args, w_gate, w_up, w_down, table)


def per_device(
    hidden_rows, expert_ids, route_weights, w_gate, w_up, w_down,
    codes, owner_slot, code_table, conv_state, conv_taps, conv_bias, upsample,
):
    n_e = lax.axis_size("expert")
    width = hidden_rows.shape[2]
    experts = n_e * w_gate.shape[0]
    books, shard, channels = code_table.shape
    results = exchange(
        (
            hidden_rows, expert_ids.transpose(1, 2, 0), route_weights.transpose(1, 2, 0), codes,
            owner_slot.reshape(1, -1), conv_state.transpose(1, 0, 2), conv_taps, conv_bias.reshape(1, -1), upsample,
        ),
        w_gate, w_up, w_down.reshape(-1, width), code_table.reshape(books * shard, channels),
        experts, books,
    )
    vm_spec = pl.BlockSpec(memory_space=pltpu.VMEM)
    moe, samples, carried = pl.pallas_call(
        hand_over,
        out_shape=tuple(jax.ShapeDtypeStruct(r.shape, r.dtype) for r in results),
        in_specs=[vm_spec] * 3,
        out_specs=(vm_spec,) * 3,
    )(*results)
    return moe, samples, carried.transpose(1, 0, 2)


def solution(mesh):
    rows = P(("groups", "expert", "wave"), None, None)
    placed = (
        rows, rows, rows,
        P("expert", None, "wave"), P("expert", None, "wave"), P("expert", "wave", None),
        rows, P(("groups", "expert", "wave")), P(None, "expert", None), rows, P(), P(), P(),
    )
    return jax.shard_map(
        per_device, mesh=mesh, in_specs=placed, out_specs=(rows, rows, rows), check_vma=False
    )
```

```python
import functools

import jax
import jax.numpy as jnp
from jax import lax
from jax.experimental import pallas as pl
from jax.experimental.pallas import tpu as pltpu
from jax.sharding import PartitionSpec as P

MESH = pl.DeviceIdType.MESH
BF = jnp.bfloat16
F32 = jnp.float32
RADIX = 64
LANES = 128
INNER = 2
HALVES = 2


def dot(a, b):
    return jnp.dot(a, b, preferred_element_type=F32)


def kernel(
    n_e, experts, books,
    h_ref, id_ref, rw_ref, co_ref, ow_ref, st_ref, tap_ref, bias_ref, us_ref,
    wg_ref, wu_ref, wd_ref, tab_ref,
    moe_ref, wave_ref, new_ref,
    hv, idv, rwv, cov, owv, stv, tapv, biasv, usv,
    xg, meta, wgu, wdv, tabv, mem, act, early, told, po, pn, my, ma, mz, mine,
    fs, fy, fa, fz, gz, ga, gy, fr,
    in_sem, w_sem, pws, pwr, zus, zds, yss, agr, mes, mer,
    mys, myr, mzs, mzr, fys, fyr, fzs, fzr, gzs, gzr, gys, below, above, aside,
):
    outer = n_e // INNER
    sessions, steps, width = hv.shape
    rows = sessions * steps
    channels = tab_ref.shape[1]
    local, _, units = wg_ref.shape
    ff = 2 * units
    shard = tab_ref.shape[0] // books
    wave_rows = n_e * rows
    col_rows = outer * rows
    e = lax.axis_index("expert")
    w = lax.axis_index("wave")
    z = e // INNER
    y = e % INNER
    peer = 1 - w
    ye = z * INNER + (1 - y)
    low = z < outer // 2

    def remote(src, dst, ssem, rsem, te, tw):
        return pltpu.make_async_remote_copy(
            src_ref=src, dst_ref=dst, send_sem=ssem, recv_sem=rsem,
            device_id={"expert": te, "wave": tw}, device_id_type=MESH,
        )

    barrier = pltpu.get_barrier_semaphore()

    def greet(te, tw):
        pl.semaphore_signal(barrier, inc=1, device_id={"expert": te, "wave": tw}, device_id_type=MESH)

    greet(e, peer)
    greet(ye, w)

    @pl.when(z > 0)
    def _():
        greet(e - INNER, w)

    @pl.when(z < outer - 1)
    def _():
        greet(e + INNER, w)

    firsts = [
        pltpu.make_async_copy(src, dst, in_sem.at[i])
        for i, (src, dst) in enumerate((
            (h_ref, hv), (id_ref, idv), (rw_ref, rwv), (co_ref, cov), (ow_ref, owv),
            (st_ref, stv), (tap_ref, tapv), (bias_ref, biasv), (us_ref, usv),
        ))
    ]
    for copy in firsts[:5]:
        copy.start()

    def gate_at(tw):
        return pl.ds(pl.multiple_of(tw * units, LANES), units)

    def up_at(tw):
        return pl.ds(pl.multiple_of(ff + tw * units, LANES), units)

    def down_at(j, tw):
        return pl.ds(pl.multiple_of(j * ff + tw * units, LANES), units)

    def weights(tw):
        pairs = []
        for j in range(local):
            pairs.append((wg_ref.at[j], wgu.at[j, :, gate_at(tw)]))
            pairs.append((wu_ref.at[j], wgu.at[j, :, up_at(tw)]))
        for j in range(local):
            pairs.append((wd_ref.at[pl.ds(j * units, units), :], wdv.at[down_at(j, tw), :]))
        return pairs

    loads = [
        pltpu.make_async_copy(src, dst, w_sem.at[i]) for i, (src, dst) in enumerate(weights(w))
    ]
    table = pltpu.make_async_copy(tab_ref, tabv, w_sem.at[3 * local])
    gives = [
        remote(src, dst, pws.at[i], pwr.at[i], e, peer) for i, (src, dst) in enumerate(weights(w))
    ]
    takes = [
        remote(src, dst, pws.at[i], pwr.at[i], e, peer) for i, (src, dst) in enumerate(weights(peer))
    ]

    half = rows // HALVES

    def at(rel, zo, p):
        return pl.ds(pl.multiple_of((rel * outer + zo) * rows + p * half, half), half)

    def agsem(rel, zo, p):
        return agr.at[(rel * outer + zo) * HALVES + p]

    def up(zo, p):
        s = xg.at[at(0, zo, p), :]
        return remote(s, s, zus.at[zo * HALVES + p], agsem(0, zo, p), (z + 1) * INNER + y, w)

    def down(zo, p):
        s = xg.at[at(0, zo, p), :]
        return remote(s, s, zds.at[zo * HALVES + p], agsem(0, zo, p), (z - 1) * INNER + y, w)

    def across(zo, p):
        return remote(
            xg.at[at(0, zo, p), :], xg.at[at(1, zo, p), :], yss.at[zo * HALVES + p], agsem(1, zo, p), ye, w
        )

    def arrived(rel, zo, p):
        s = xg.at[at(rel, zo, p), :]
        remote(s, s, yss.at[0], agsem(rel, zo, p), ye, w).wait_recv()

    def meta_at(te, se):
        rel = (te % INNER + se % INNER) % 2
        return pl.ds(pl.multiple_of((rel * outer + se // INNER) * rows, rows), rows)

    def tell(d):
        te = (e + d) % n_e
        return remote(
            meta.at[meta_at(e, e), :], meta.at[meta_at(te, e), :], mes.at[d - 1], mer.at[d - 1], te, w
        )

    def told_by(d):
        se = (e - d + n_e) % n_e
        s = meta.at[meta_at(e, se), :]
        return remote(s, s, mes.at[d - 1], mer.at[d - 1], se, w)

    firsts[0].wait()
    hid = hv[...]
    mine_at = pl.multiple_of(z * rows, rows)
    for t in range(steps):
        xg[pl.ds(mine_at + t * sessions, sessions), :] = hid[:, t, :]
    for copy in firsts[5:]:
        copy.start()
    table.start()
    for load in loads:
        load.start()
    pl.semaphore_wait(barrier, 2 + (z > 0).astype(jnp.int32) + (z < outer - 1).astype(jnp.int32))

    for p in range(HALVES):
        @pl.when(z + 1 < outer)
        def _():
            up(z, p).start()

        @pl.when(z > 0)
        def _():
            down(z, p).start()

        across(z, p).start()
    for give in gives:
        give.start()

    lanes = meta.shape[1]
    dest_at = 2 * experts
    code_at = dest_at + 8

    def placed(count, start):
        here = lax.broadcasted_iota(jnp.int32, (count, lanes), 0)
        there = lax.broadcasted_iota(jnp.int32, (count, lanes), 1)
        return jnp.where(here + start == there, 1.0, 0.0).astype(BF)

    for copy in firsts[1:5]:
        copy.wait()
    owner = owv[...].astype(F32)
    holder = jnp.floor((owner + 0.5) / sessions)
    within = owner - holder * sessions
    holder = jnp.floor((holder + 0.5) / 2)
    expert_i = lax.broadcasted_iota(jnp.int32, (experts, sessions), 0)
    digit = lax.broadcasted_iota(jnp.int32, (8, sessions), 0)
    for t in range(steps):
        both = jnp.zeros((experts, sessions), F32)
        for k in range(idv.shape[1]):
            both += jnp.where(expert_i == idv[t, k:k + 1, :], rwv[t, k:k + 1, :], 0.0)
        high = both.astype(BF).astype(F32)
        dest = holder * rows + t * sessions + within
        top = jnp.floor((dest + 0.5) / RADIX)
        digits = jnp.where(digit == 0, top, jnp.where(digit == 1, dest - top * RADIX, 0.0))
        upright = jnp.concatenate([high, both - high, digits], axis=0).astype(BF)
        extra = lax.dot_general(
            upright, placed(code_at, 0), (((0,), (0,)), ((), ())), preferred_element_type=F32
        )
        co = cov[:, t, :].astype(F32)
        top = jnp.floor((co + 0.5) / RADIX)
        extra += dot(top.astype(BF), placed(books, code_at))
        extra += dot((co - top * RADIX).astype(BF), placed(books, code_at + books))
        meta[pl.ds(mine_at + t * sessions, sessions), :] = extra.astype(BF)

    def signal(sem, te):
        pl.semaphore_signal(sem, inc=1, device_id={"expert": te, "wave": w}, device_id_type=MESH)

    def upward():
        @pl.when(z > 0)
        def _():
            pl.semaphore_wait(below, 1)

        @pl.when(z < outer - 1)
        def _():
            signal(below, e + INNER)

    def downward():
        @pl.when(z < outer - 1)
        def _():
            pl.semaphore_wait(above, 1)

        @pl.when(z > 0)
        def _():
            signal(above, e - INNER)

    @pl.when(low)
    def _():
        upward()
        downward()

    @pl.when(jnp.logical_not(low))
    def _():
        downward()
        upward()

    signal(aside, ye)
    pl.semaphore_wait(aside, 1)
    for d in range(1, n_e):
        tell(d).start()

    for copy in firsts[5:]:
        copy.wait()
    state_len = stv.shape[0]
    taps = tapv.shape[0]

    def before():
        for t in range(steps):
            total = jnp.broadcast_to(biasv[...], (sessions, channels))
            for j in range(t + 1, taps):
                total += tapv[j:j + 1, :] * stv[state_len + t - j].astype(F32)
            early[t * sessions:(t + 1) * sessions, :] = total
        for i in range(state_len - steps):
            new_ref[i] = stv[i + steps]

    def forward(step):
        for p in range(HALVES):
            @pl.when(z - step >= 0)
            def _():
                zo = z - step
                arrived(0, zo, p)

                @pl.when(z + 1 < outer)
                def _():
                    up(zo, p).start()

                across(zo, p).start()

            @pl.when(z + step < outer)
            def _():
                zo = z + step
                arrived(0, zo, p)

                @pl.when(z > 0)
                def _():
                    down(zo, p).start()

                across(zo, p).start()

    src = lax.broadcasted_iota(jnp.int32, (lanes, LANES), 0)
    col = lax.broadcasted_iota(jnp.int32, (lanes, LANES), 1)

    def learn():
        for d in range(1, n_e):
            told_by(d).wait_recv()
        is_code = col < books
        pick = jnp.where(is_code & (src == code_at + col), float(RADIX), 0.0)
        pick += jnp.where(is_code & (src == code_at + books + col), 1.0, 0.0)
        pick += jnp.where((col == books) & (src == dest_at), float(RADIX), 0.0)
        pick += jnp.where((col == books) & (src == dest_at + 1), 1.0, 0.0)
        own = e * local + col - (books + 1)
        is_weight = (col > books) & (col <= books + local)
        pick += jnp.where(is_weight & ((src == own) | (src == own + experts)), 1.0, 0.0)
        told[...] = dot(meta[...], pick.astype(BF))
        lane = lax.broadcasted_iota(jnp.int32, (wave_rows, shard), 1).astype(F32)
        first = (e * shard).astype(F32)
        for q in range(books):
            mem[:, q * shard:(q + 1) * shard] = jnp.where(
                told[:, q:q + 1] - first == lane, 1.0, 0.0
            ).astype(BF)

    def embed():
        place = lax.broadcasted_iota(jnp.int32, (wave_rows, wave_rows), 1).astype(F32)
        order = jnp.where(told[:, books:books + 1] == place, 1.0, 0.0).astype(BF)
        table.wait()
        f_tile = min(channels, 512)

        @pl.loop(0, channels // f_tile)
        def _(n):
            cols = pl.ds(pl.multiple_of(n * f_tile, f_tile), f_tile)
            part = dot(mem[...], tabv[:, cols]).astype(BF)
            fs[:, cols] = lax.dot_general(
                order, part, (((0,), (0,)), ((), ())), preferred_element_type=F32
            ).astype(BF)

    def goal(k):
        if k == outer - 1:
            return z
        down_from = outer - 1 - k
        down_from = down_from - (down_from <= z).astype(jnp.int32)
        up_from = k + (k >= z).astype(jnp.int32)
        return jnp.where(low, down_from, up_from)

    def block(zo, yo):
        return pl.ds(pl.multiple_of((zo * INNER + yo) * rows, rows), rows)

    def zrows(zo):
        return pl.ds(pl.multiple_of(zo * rows, rows), rows)

    def hop(zo):
        return (zo - z + outer) % outer - 1

    split = channels // 2
    first_half = pl.ds(0, split)
    second_half = pl.ds(split, split)

    def pair(zo):
        return pl.ds(pl.multiple_of(zo * INNER * rows, INNER * rows), INNER * rows)

    def fy_copy(zo):
        return remote(fs.at[block(zo, 1 - y), first_half], fy.at[zrows(zo), :], fys.at[zo], fyr.at[zo], ye, w)

    def fz_copy(zo):
        d = hop(zo)
        return remote(fa.at[zrows(zo), :], fz.at[zrows(d), :], fzs.at[d], fzr.at[d], zo * INNER + y, w)

    def fz_got(d):
        s = fz.at[zrows(d), :]
        return remote(s, s, fzs.at[d], fzr.at[d], ye, w)

    def gz_copy(zo):
        d = hop(zo)
        return remote(fs.at[pair(zo), second_half], gz.at[pair(d), :], gzs.at[d], gzr.at[d], zo * INNER + y, w)

    def gz_got(d):
        s = gz.at[pair(d), :]
        return remote(s, s, gzs.at[d], gzr.at[d], ye, w)

    def gy_copy():
        return remote(ga, gy, gys.at[0], gys.at[1], ye, w)

    part_cols = width // HALVES

    def cols_of(p):
        return pl.ds(p * part_cols, part_cols)

    def my_copy(zo, p):
        i = zo * HALVES + p
        return remote(
            pn.at[zrows(zo), cols_of(p)], my.at[zrows(zo), cols_of(p)], mys.at[i], myr.at[i], ye, w
        )

    def mz_copy(zo, p):
        there = (z - zo + outer) % outer
        return remote(
            ma.at[zrows(zo), cols_of(p)], mz.at[zrows(there), cols_of(p)],
            mzs.at[zo * HALVES + p], mzr.at[there * HALVES + p], zo * INNER + y, w,
        )

    def mz_got(there, p):
        s = mz.at[zrows(there), cols_of(p)]
        return remote(s, s, mzs.at[0], mzr.at[there * HALVES + p], ye, w)

    rc = min(col_rows, 128)

    def looped(count, body):
        if count == 1:
            body(0)
        else:
            pl.loop(0, count)(body)

    def ready(i):
        loads[i].wait()
        takes[i].wait_recv()

    def hidden(rel, j):
        def piece(i):
            here = pl.ds(pl.multiple_of(rel * col_rows + i * rc, rc), rc)
            x = xg[here, :]
            weight = told[here, books + 1 + j:books + 2 + j]
            tile = ff // 3 if ff % (3 * LANES) == 0 else ff
            for n in range(0, ff, tile):
                g = dot(x, wgu[j, :, n:n + tile])
                u = dot(x, wgu[j, :, ff + n:ff + n + tile])
                a = g / (1.0 + jnp.exp(-g)) * u * weight
                act[here, j * ff + n:j * ff + n + tile] = a.astype(BF)

        looped(col_rows // rc, piece)

    def project(rel, dst, p):
        def piece(i):
            here = pl.ds(pl.multiple_of(rel * col_rows + i * rc, rc), rc)
            there = pl.ds(pl.multiple_of(i * rc, rc), rc)
            tile = min(part_cols, 512)
            for n in range(p * part_cols, (p + 1) * part_cols, tile):
                dst[there, n:n + tile] = dot(act[here, :], wdv[:, n:n + tile]).astype(BF)

        looped(col_rows // rc, piece)

    def frames_on(k):
        zo = goal(k)
        total = fs[block(zo, y), first_half].astype(F32)
        fy_copy(zo).wait_recv()
        total += fy[zrows(zo), :].astype(F32)
        if k < outer - 1:
            fa[zrows(zo), :] = total.astype(BF)
            fz_copy(zo).start()
        else:
            fr[:, first_half] = total

    before()
    for step in range(1, outer):
        forward(step)
        if step == 1:
            learn()
        if step == min(2, outer - 1):
            embed()
    for k in range(outer - 1):
        gz_copy(goal(k)).start()
    for k in range(outer):
        fy_copy(goal(k)).start()

    def both_ready(j):
        ready(2 * j)
        ready(2 * j + 1)

    both_ready(0)
    hidden(0, 0)
    for zo in range(outer):
        for p in range(HALVES):
            arrived(1, zo, p)
    for j in range(local):
        if j > 0:
            both_ready(j)
        hidden(1, j)
        if j < outer - 1:
            frames_on(j)
    for j in range(local):
        ready(2 * local + j)
    for p in range(HALVES):
        project(1, pn, p)
        my_copy(goal(0), p).start()
    for k in range(1, outer - 1):
        for p in range(HALVES):
            my_copy(goal(k), p).start()
    for k in range(min(local, outer - 1), outer):
        frames_on(k)
    for j in range(1, local):
        hidden(0, j)
    for p in range(HALVES):
        project(0, po, p)

    def frames_across():
        there = fs[block(z, 1 - y), second_half].astype(F32)
        here = fs[block(z, y), second_half].astype(F32)
        for d in range(outer - 1):
            gz_got(d).wait_recv()
            start = pl.multiple_of(d * INNER * rows, rows)
            there += gz[pl.ds(start + (1 - y) * rows, rows), :].astype(F32)
            here += gz[pl.ds(start + y * rows, rows), :].astype(F32)
        ga[...] = there.astype(BF)
        gy_copy().start()
        fr[:, second_half] = here

    def pass_on(k):
        zo = goal(k)
        for p in range(HALVES):
            my_copy(zo, p).wait_recv()
            here = (zrows(zo), cols_of(p))
            ma[here] = (po[here].astype(F32) + my[here].astype(F32)).astype(BF)
            mz_copy(zo, p).start()

    def finish_frames():
        for d in range(outer - 1):
            fz_got(d).wait_recv()
            fr[:, first_half] += fz[zrows(d), :].astype(F32)
        gy_copy().wait_recv()
        fr[:, second_half] += gy[...].astype(F32)
        got = [fr[t * sessions:(t + 1) * sessions, :] for t in range(steps)]
        decoded = []
        for t in range(steps):
            total = early[t * sessions:(t + 1) * sessions, :]
            for j in range(t + 1):
                total += tapv[j:j + 1, :] * got[t - j]
            decoded.append(jax.nn.gelu(total).astype(BF))
            new_ref[state_len - steps + t] = got[t].astype(BF)
        samples = dot(jnp.concatenate(decoded, axis=0), usv[...]).astype(BF)
        for t in range(steps):
            wave_ref[:, t, :] = samples[t * sessions:(t + 1) * sessions]

    pass_on(0)
    frames_across()
    for p in range(HALVES):
        my_copy(z, p).start()
    for k in range(1, outer - 1):
        pass_on(k)
    finish_frames()
    for p in range(HALVES):
        my_copy(z, p).wait_recv()
        mine[...] = po[zrows(z), cols_of(p)].astype(F32) + my[zrows(z), cols_of(p)].astype(F32)

        for d in range(1, outer):
            mz_got(d, p).wait_recv()
            mine[...] += mz[zrows(d), cols_of(p)].astype(F32)

        for t in range(steps):
            moe_ref[:, t, p * part_cols:(p + 1) * part_cols] = mine[t * sessions:(t + 1) * sessions, :].astype(BF)

    gy_copy().wait_send()
    for give in gives:
        give.wait_send()
    for d in range(1, n_e):
        tell(d).wait_send()
    for zo in range(outer):
        for p in range(HALVES):
            @pl.when((z + 1 < outer) & (zo <= z))
            def _():
                up(zo, p).wait_send()

            @pl.when((z > 0) & (zo >= z))
            def _():
                down(zo, p).wait_send()

            across(zo, p).wait_send()
            my_copy(zo, p).wait_send()
        fy_copy(zo).wait_send()
    for k in range(outer - 1):
        zo = goal(k)
        fz_copy(zo).wait_send()
        gz_copy(zo).wait_send()
        for p in range(HALVES):
            mz_copy(zo, p).wait_send()


def hand_over(a_ref, b_ref, c_ref, a_out, b_out, c_out, sems):
    copies = [
        pltpu.make_async_copy(src, dst, sems.at[i])
        for i, (src, dst) in enumerate(((a_ref, a_out), (b_ref, b_out), (c_ref, c_out)))
    ]
    for copy in copies:
        copy.start()
    for copy in copies:
        copy.wait()


def exchange(args, w_gate, w_up, w_down, table, experts, books):
    n_e = lax.axis_size("expert")
    outer = n_e // INNER
    sessions, steps, width = args[0].shape
    rows = sessions * steps
    used = 2 * experts + 8 + 2 * books
    lanes = used + -used % LANES
    local, _, units = w_gate.shape
    ff = 2 * units
    channels = table.shape[1]
    wave_rows = n_e * rows
    col_rows = outer * rows
    vm = pltpu.VMEM
    dma = lambda *s: pltpu.SemaphoreType.DMA(s)
    hops = outer - 1
    scratch = [vm(a.shape, a.dtype) for a in args] + [
        vm((wave_rows, width), BF),
        vm((wave_rows, lanes), BF),
        vm((local, width, 2 * ff), BF),
        vm((local * ff, width), BF),
        vm(table.shape, BF),
        vm((wave_rows, table.shape[0]), BF),
        vm((wave_rows, local * ff), BF),
        vm((rows, channels), F32),
        vm((wave_rows, LANES), F32),
        vm((col_rows, width), BF),
        vm((col_rows, width), BF),
        vm((col_rows, width), BF),
        vm((col_rows, width), BF),
        vm((outer * rows, width), BF),
        vm((rows, width // HALVES), F32),
        vm((wave_rows, channels), BF),
        vm((col_rows, channels // 2), BF),
        vm((col_rows, channels // 2), BF),
        vm((hops * rows, channels // 2), BF),
        vm((hops * INNER * rows, channels // 2), BF),
        vm((rows, channels // 2), BF),
        vm((rows, channels // 2), BF),
        vm((rows, channels), F32),
        dma(len(args)), dma(3 * local + 1), dma(3 * local), dma(3 * local),
        dma(outer * HALVES), dma(outer * HALVES), dma(outer * HALVES), dma(n_e * HALVES),
        dma(n_e - 1), dma(n_e - 1),
        dma(outer * HALVES), dma(outer * HALVES), dma(outer * HALVES), dma(outer * HALVES),
        dma(outer), dma(outer), dma(hops), dma(hops), dma(hops), dma(hops), dma(2),
        pltpu.SemaphoreType.REGULAR, pltpu.SemaphoreType.REGULAR, pltpu.SemaphoreType.REGULAR,
    ]
    any_spec = pl.BlockSpec(memory_space=pl.ANY)
    vm_spec = pl.BlockSpec(memory_space=pltpu.VMEM)
    return pl.pallas_call(
        functools.partial(kernel, n_e, experts, books),
        out_shape=(
            vm((sessions, steps, width), BF),
            vm((sessions, steps, args[8].shape[1]), BF),
            vm(args[5].shape, BF),
        ),
        in_specs=[any_spec] * (len(args) + 4),
        out_specs=(vm_spec, vm_spec, vm_spec),
        scratch_shapes=scratch,
        compiler_params=pltpu.CompilerParams(
            collective_id=0, has_side_effects=True, vmem_limit_bytes=60 * 1024 * 1024
        ),
    )(*args, w_gate, w_up, w_down, table)


def per_device(
    hidden_rows, expert_ids, route_weights, w_gate, w_up, w_down,
    codes, owner_slot, code_table, conv_state, conv_taps, conv_bias, upsample,
):
    n_e = lax.axis_size("expert")
    width = hidden_rows.shape[2]
    experts = n_e * w_gate.shape[0]
    books, shard, channels = code_table.shape
    results = exchange(
        (
            hidden_rows, expert_ids.transpose(1, 2, 0), route_weights.transpose(1, 2, 0), codes,
            owner_slot.reshape(1, -1), conv_state.transpose(1, 0, 2), conv_taps, conv_bias.reshape(1, -1), upsample,
        ),
        w_gate, w_up, w_down.reshape(-1, width), code_table.reshape(books * shard, channels),
        experts, books,
    )
    vm_spec = pl.BlockSpec(memory_space=pltpu.VMEM)
    moe, samples, carried = pl.pallas_call(
        hand_over,
        out_shape=tuple(jax.ShapeDtypeStruct(r.shape, r.dtype) for r in results),
        in_specs=[vm_spec] * 3,
        out_specs=(pl.BlockSpec(memory_space=pl.ANY),) * 3,
        scratch_shapes=[pltpu.SemaphoreType.DMA((3,))],
    )(*[pltpu.with_memory_space_constraint(r, pltpu.VMEM) for r in results])
    return moe, samples, carried.transpose(1, 0, 2)


def solution(mesh):
    rows = P(("groups", "expert", "wave"), None, None)
    placed = (
        rows, rows, rows,
        P("expert", None, "wave"), P("expert", None, "wave"), P("expert", "wave", None),
        rows, P(("groups", "expert", "wave")), P(None, "expert", None), rows, P(), P(), P(),
    )
    return jax.shard_map(
        per_device, mesh=mesh, in_specs=placed, out_specs=(rows, rows, rows), check_vma=False
    )
```

```python
import functools

import jax
import jax.numpy as jnp
from jax import lax
from jax.experimental import pallas as pl
from jax.experimental.pallas import tpu as pltpu
from jax.sharding import PartitionSpec as P

MESH = pl.DeviceIdType.MESH
BF = jnp.bfloat16
F32 = jnp.float32
RADIX = 64
LANES = 128
INNER = 2
HALVES = 2
PIECES = 2


def dot(a, b):
    return jnp.dot(a, b, preferred_element_type=F32)


def kernel(
    n_e, experts, books,
    h_ref, id_ref, rw_ref, co_ref, ow_ref, st_ref, tap_ref, bias_ref, us_ref,
    wg_ref, wu_ref, wd_ref, tab_ref,
    moe_ref, wave_ref, new_ref,
    hv, idv, rwv, cov, owv, stv, tapv, biasv, usv,
    xg, meta, wgu, wdv, tabv, mem, act, acc, early, told, po, pn, my, ma, mz, mine,
    fs, fy, fa, fz, gz, ga, gy, fr,
    in_sem, w_sem, pws, pwr, zus, zds, yss, agr, mes, mer,
    mys, myr, mzs, mzr, fys, fyr, fzs, fzr, gzs, gzr, gys, below, above, aside,
):
    outer = n_e // INNER
    sessions, steps, width = hv.shape
    rows = sessions * steps
    channels = tab_ref.shape[1]
    local, _, units = wg_ref.shape
    ff = 2 * units
    shard = tab_ref.shape[0] // books
    wave_rows = n_e * rows
    col_rows = outer * rows
    e = lax.axis_index("expert")
    w = lax.axis_index("wave")
    z = e // INNER
    y = e % INNER
    peer = 1 - w
    ye = z * INNER + (1 - y)
    low = z < outer // 2

    def remote(src, dst, ssem, rsem, te, tw):
        return pltpu.make_async_remote_copy(
            src_ref=src, dst_ref=dst, send_sem=ssem, recv_sem=rsem,
            device_id={"expert": te, "wave": tw}, device_id_type=MESH,
        )

    barrier = pltpu.get_barrier_semaphore()

    def greet(te, tw):
        pl.semaphore_signal(barrier, inc=1, device_id={"expert": te, "wave": tw}, device_id_type=MESH)

    greet(e, peer)
    greet(ye, w)

    @pl.when(z > 0)
    def _():
        greet(e - INNER, w)

    @pl.when(z < outer - 1)
    def _():
        greet(e + INNER, w)

    firsts = [
        pltpu.make_async_copy(src, dst, in_sem.at[i])
        for i, (src, dst) in enumerate((
            (h_ref, hv), (id_ref, idv), (rw_ref, rwv), (co_ref, cov), (ow_ref, owv),
            (st_ref, stv), (tap_ref, tapv), (bias_ref, biasv), (us_ref, usv),
        ))
    ]
    for copy in firsts[:5]:
        copy.start()

    def gate_at(tw):
        return pl.ds(pl.multiple_of(tw * units, LANES), units)

    def up_at(tw):
        return pl.ds(pl.multiple_of(ff + tw * units, LANES), units)

    def down_at(j, tw):
        return pl.ds(pl.multiple_of(j * ff + tw * units, LANES), units)

    def weights(tw):
        pairs = []
        for j in range(local):
            pairs.append((wg_ref.at[j], wgu.at[j, :, gate_at(tw)]))
            pairs.append((wu_ref.at[j], wgu.at[j, :, up_at(tw)]))
        for j in range(local):
            pairs.append((wd_ref.at[pl.ds(j * units, units), :], wdv.at[down_at(j, tw), :]))
        return pairs

    loads = [
        pltpu.make_async_copy(src, dst, w_sem.at[i]) for i, (src, dst) in enumerate(weights(w))
    ]
    table = pltpu.make_async_copy(tab_ref, tabv, w_sem.at[3 * local])
    gives = [
        remote(src, dst, pws.at[i], pwr.at[i], e, peer) for i, (src, dst) in enumerate(weights(w))
    ]
    takes = [
        remote(src, dst, pws.at[i], pwr.at[i], e, peer) for i, (src, dst) in enumerate(weights(peer))
    ]

    piece_cols = width // PIECES

    def at(rel, zo, p):
        return (
            pl.ds(pl.multiple_of((rel * outer + zo) * rows, rows), rows), pl.ds(p * piece_cols, piece_cols)
        )

    def agsem(rel, zo, p):
        return agr.at[(rel * outer + zo) * PIECES + p]

    def up(zo, p):
        s = xg.at[at(0, zo, p)]
        return remote(s, s, zus.at[zo * PIECES + p], agsem(0, zo, p), (z + 1) * INNER + y, w)

    def down(zo, p):
        s = xg.at[at(0, zo, p)]
        return remote(s, s, zds.at[zo * PIECES + p], agsem(0, zo, p), (z - 1) * INNER + y, w)

    def across(zo, p):
        return remote(
            xg.at[at(0, zo, p)], xg.at[at(1, zo, p)], yss.at[zo * PIECES + p], agsem(1, zo, p), ye, w
        )

    def arrived(rel, zo, p):
        s = xg.at[at(rel, zo, p)]
        remote(s, s, yss.at[0], agsem(rel, zo, p), ye, w).wait_recv()

    def meta_at(te, se):
        rel = (te % INNER + se % INNER) % 2
        return pl.ds(pl.multiple_of((rel * outer + se // INNER) * rows, rows), rows)

    def tell(d):
        te = (e + d) % n_e
        return remote(
            meta.at[meta_at(e, e), :], meta.at[meta_at(te, e), :], mes.at[d - 1], mer.at[d - 1], te, w
        )

    def told_by(d):
        se = (e - d + n_e) % n_e
        s = meta.at[meta_at(e, se), :]
        return remote(s, s, mes.at[d - 1], mer.at[d - 1], se, w)

    firsts[0].wait()
    hid = hv[...]
    mine_at = pl.multiple_of(z * rows, rows)
    for t in range(steps):
        xg[pl.ds(mine_at + t * sessions, sessions), :] = hid[:, t, :]
    for copy in firsts[5:]:
        copy.start()
    table.start()
    for load in loads:
        load.start()
    pl.semaphore_wait(barrier, 2 + (z > 0).astype(jnp.int32) + (z < outer - 1).astype(jnp.int32))

    for p in range(PIECES):
        @pl.when(z + 1 < outer)
        def _():
            up(z, p).start()

        @pl.when(z > 0)
        def _():
            down(z, p).start()

        across(z, p).start()
    for give in gives:
        give.start()

    lanes = meta.shape[1]
    dest_at = 2 * experts
    code_at = dest_at + 8

    def placed(count, start):
        here = lax.broadcasted_iota(jnp.int32, (count, lanes), 0)
        there = lax.broadcasted_iota(jnp.int32, (count, lanes), 1)
        return jnp.where(here + start == there, 1.0, 0.0).astype(BF)

    for copy in firsts[1:5]:
        copy.wait()
    owner = owv[...].astype(F32)
    holder = jnp.floor((owner + 0.5) / sessions)
    within = owner - holder * sessions
    holder = jnp.floor((holder + 0.5) / 2)
    expert_i = lax.broadcasted_iota(jnp.int32, (experts, sessions), 0)
    digit = lax.broadcasted_iota(jnp.int32, (8, sessions), 0)
    for t in range(steps):
        both = jnp.zeros((experts, sessions), F32)
        for k in range(idv.shape[1]):
            both += jnp.where(expert_i == idv[t, k:k + 1, :], rwv[t, k:k + 1, :], 0.0)
        high = both.astype(BF).astype(F32)
        dest = holder * rows + t * sessions + within
        top = jnp.floor((dest + 0.5) / RADIX)
        digits = jnp.where(digit == 0, top, jnp.where(digit == 1, dest - top * RADIX, 0.0))
        upright = jnp.concatenate([high, both - high, digits], axis=0).astype(BF)
        extra = lax.dot_general(
            upright, placed(code_at, 0), (((0,), (0,)), ((), ())), preferred_element_type=F32
        )
        co = cov[:, t, :].astype(F32)
        top = jnp.floor((co + 0.5) / RADIX)
        extra += dot(top.astype(BF), placed(books, code_at))
        extra += dot((co - top * RADIX).astype(BF), placed(books, code_at + books))
        meta[pl.ds(mine_at + t * sessions, sessions), :] = extra.astype(BF)

    def signal(sem, te):
        pl.semaphore_signal(sem, inc=1, device_id={"expert": te, "wave": w}, device_id_type=MESH)

    def upward():
        @pl.when(z > 0)
        def _():
            pl.semaphore_wait(below, 1)

        @pl.when(z < outer - 1)
        def _():
            signal(below, e + INNER)

    def downward():
        @pl.when(z < outer - 1)
        def _():
            pl.semaphore_wait(above, 1)

        @pl.when(z > 0)
        def _():
            signal(above, e - INNER)

    @pl.when(low)
    def _():
        upward()
        downward()

    @pl.when(jnp.logical_not(low))
    def _():
        downward()
        upward()

    signal(aside, ye)
    pl.semaphore_wait(aside, 1)
    for d in range(1, n_e):
        tell(d).start()

    for copy in firsts[5:]:
        copy.wait()
    state_len = stv.shape[0]
    taps = tapv.shape[0]

    def before():
        for t in range(steps):
            total = jnp.broadcast_to(biasv[...], (sessions, channels))
            for j in range(t + 1, taps):
                total += tapv[j:j + 1, :] * stv[state_len + t - j].astype(F32)
            early[t * sessions:(t + 1) * sessions, :] = total
        for i in range(state_len - steps):
            new_ref[i] = stv[i + steps]

    def forward(step):
        for p in range(PIECES):
            @pl.when(z - step >= 0)
            def _():
                zo = z - step
                arrived(0, zo, p)

                @pl.when(z + 1 < outer)
                def _():
                    up(zo, p).start()

                across(zo, p).start()

            @pl.when(z + step < outer)
            def _():
                zo = z + step
                arrived(0, zo, p)

                @pl.when(z > 0)
                def _():
                    down(zo, p).start()

                across(zo, p).start()

    src = lax.broadcasted_iota(jnp.int32, (lanes, LANES), 0)
    col = lax.broadcasted_iota(jnp.int32, (lanes, LANES), 1)

    def learn():
        for d in range(1, n_e):
            told_by(d).wait_recv()
        is_code = col < books
        pick = jnp.where(is_code & (src == code_at + col), float(RADIX), 0.0)
        pick += jnp.where(is_code & (src == code_at + books + col), 1.0, 0.0)
        pick += jnp.where((col == books) & (src == dest_at), float(RADIX), 0.0)
        pick += jnp.where((col == books) & (src == dest_at + 1), 1.0, 0.0)
        own = e * local + col - (books + 1)
        is_weight = (col > books) & (col <= books + local)
        pick += jnp.where(is_weight & ((src == own) | (src == own + experts)), 1.0, 0.0)
        told[...] = dot(meta[...], pick.astype(BF))
        lane = lax.broadcasted_iota(jnp.int32, (wave_rows, shard), 1).astype(F32)
        first = (e * shard).astype(F32)
        for q in range(books):
            mem[:, q * shard:(q + 1) * shard] = jnp.where(
                told[:, q:q + 1] - first == lane, 1.0, 0.0
            ).astype(BF)

    def embed():
        place = lax.broadcasted_iota(jnp.int32, (wave_rows, wave_rows), 1).astype(F32)
        order = jnp.where(told[:, books:books + 1] == place, 1.0, 0.0).astype(BF)
        table.wait()
        f_tile = min(channels, 512)

        @pl.loop(0, channels // f_tile)
        def _(n):
            cols = pl.ds(pl.multiple_of(n * f_tile, f_tile), f_tile)
            part = dot(mem[...], tabv[:, cols]).astype(BF)
            fs[:, cols] = lax.dot_general(
                order, part, (((0,), (0,)), ((), ())), preferred_element_type=F32
            ).astype(BF)

    def goal(k):
        if k == outer - 1:
            return z
        down_from = outer - 1 - k
        down_from = down_from - (down_from <= z).astype(jnp.int32)
        up_from = k + (k >= z).astype(jnp.int32)
        return jnp.where(low, down_from, up_from)

    def block(zo, yo):
        return pl.ds(pl.multiple_of((zo * INNER + yo) * rows, rows), rows)

    def zrows(zo):
        return pl.ds(pl.multiple_of(zo * rows, rows), rows)

    def hop(zo):
        return (zo - z + outer) % outer - 1

    split = channels // 2
    first_half = pl.ds(0, split)
    second_half = pl.ds(split, split)

    def pair(zo):
        return pl.ds(pl.multiple_of(zo * INNER * rows, INNER * rows), INNER * rows)

    def fy_copy(zo):
        return remote(fs.at[block(zo, 1 - y), first_half], fy.at[zrows(zo), :], fys.at[zo], fyr.at[zo], ye, w)

    def fz_copy(zo):
        d = hop(zo)
        return remote(fa.at[zrows(zo), :], fz.at[zrows(d), :], fzs.at[d], fzr.at[d], zo * INNER + y, w)

    def fz_got(d):
        s = fz.at[zrows(d), :]
        return remote(s, s, fzs.at[d], fzr.at[d], ye, w)

    def gz_copy(zo):
        d = hop(zo)
        return remote(fs.at[pair(zo), second_half], gz.at[pair(d), :], gzs.at[d], gzr.at[d], zo * INNER + y, w)

    def gz_got(d):
        s = gz.at[pair(d), :]
        return remote(s, s, gzs.at[d], gzr.at[d], ye, w)

    def gy_copy():
        return remote(ga, gy, gys.at[0], gys.at[1], ye, w)

    part_cols = width // HALVES

    def cols_of(p):
        return pl.ds(p * part_cols, part_cols)

    def my_copy(zo, p):
        i = zo * HALVES + p
        return remote(
            pn.at[zrows(zo), cols_of(p)], my.at[zrows(zo), cols_of(p)], mys.at[i], myr.at[i], ye, w
        )

    def mz_copy(zo, p):
        there = (z - zo + outer) % outer
        return remote(
            ma.at[zrows(zo), cols_of(p)], mz.at[zrows(there), cols_of(p)],
            mzs.at[zo * HALVES + p], mzr.at[there * HALVES + p], zo * INNER + y, w,
        )

    def mz_got(there, p):
        s = mz.at[zrows(there), cols_of(p)]
        return remote(s, s, mzs.at[0], mzr.at[there * HALVES + p], ye, w)

    rc = min(col_rows, 128)
    early_cols = width - piece_cols

    def looped(count, body):
        if count == 1:
            body(0)
        else:
            pl.loop(0, count)(body)

    def ready(i):
        loads[i].wait()
        takes[i].wait_recv()

    def hidden(rel, j):
        def piece(i):
            here = pl.ds(pl.multiple_of(rel * col_rows + i * rc, rc), rc)
            x = xg[here, :]
            weight = told[here, books + 1 + j:books + 2 + j]
            tile = ff // 3 if ff % (3 * LANES) == 0 else ff
            for n in range(0, ff, tile):
                g = dot(x, wgu[j, :, n:n + tile])
                u = dot(x, wgu[j, :, ff + n:ff + n + tile])
                a = g / (1.0 + jnp.exp(-g)) * u * weight
                act[here, j * ff + n:j * ff + n + tile] = a.astype(BF)

        looped(col_rows // rc, piece)

    def hidden_start(j):
        def piece(i):
            here = pl.ds(pl.multiple_of(col_rows + i * rc, rc), rc)
            there = pl.ds(pl.multiple_of(i * rc, rc), rc)
            x = xg[here, :early_cols]
            tile = 2 * ff // 3 if ff % (3 * LANES) == 0 else ff
            for n in range(0, 2 * ff, tile):
                acc[there, j * 2 * ff + n:j * 2 * ff + n + tile] = dot(x, wgu[j, :early_cols, n:n + tile])

        looped(col_rows // rc, piece)

    def hidden_end(j):
        def piece(i):
            here = pl.ds(pl.multiple_of(col_rows + i * rc, rc), rc)
            there = pl.ds(pl.multiple_of(i * rc, rc), rc)
            x = xg[here, early_cols:]
            weight = told[here, books + 1 + j:books + 2 + j]
            tile = ff // 3 if ff % (3 * LANES) == 0 else ff
            for n in range(0, ff, tile):
                base = j * 2 * ff + n
                g = acc[there, base:base + tile] + dot(x, wgu[j, early_cols:, n:n + tile])
                u = acc[there, base + ff:base + ff + tile] + dot(x, wgu[j, early_cols:, ff + n:ff + n + tile])
                a = g / (1.0 + jnp.exp(-g)) * u * weight
                act[here, j * ff + n:j * ff + n + tile] = a.astype(BF)

        looped(col_rows // rc, piece)

    def project(rel, dst, p):
        def piece(i):
            here = pl.ds(pl.multiple_of(rel * col_rows + i * rc, rc), rc)
            there = pl.ds(pl.multiple_of(i * rc, rc), rc)
            tile = min(part_cols, 512)
            for n in range(p * part_cols, (p + 1) * part_cols, tile):
                dst[there, n:n + tile] = dot(act[here, :], wdv[:, n:n + tile]).astype(BF)

        looped(col_rows // rc, piece)

    def frames_on(k):
        zo = goal(k)
        total = fs[block(zo, y), first_half].astype(F32)
        fy_copy(zo).wait_recv()
        total += fy[zrows(zo), :].astype(F32)
        if k < outer - 1:
            fa[zrows(zo), :] = total.astype(BF)
            fz_copy(zo).start()
        else:
            fr[:, first_half] = total

    before()
    for step in range(1, outer):
        forward(step)
        if step == 1:
            learn()
        if step == min(2, outer - 1):
            embed()
    for k in range(outer - 1):
        gz_copy(goal(k)).start()
    for k in range(outer):
        fy_copy(goal(k)).start()

    def both_ready(j):
        ready(2 * j)
        ready(2 * j + 1)

    both_ready(0)
    hidden(0, 0)
    for zo in range(outer):
        for p in range(PIECES - 1):
            arrived(1, zo, p)
    for j in range(local):
        if j > 0:
            both_ready(j)
        hidden_start(j)
    for zo in range(outer):
        arrived(1, zo, PIECES - 1)
    for j in range(local):
        hidden_end(j)
        if j < outer - 1:
            frames_on(j)
    for j in range(local):
        ready(2 * local + j)
    for p in range(HALVES):
        project(1, pn, p)
        my_copy(goal(0), p).start()
    for k in range(1, outer - 1):
        for p in range(HALVES):
            my_copy(goal(k), p).start()
    for k in range(min(local, outer - 1), outer):
        frames_on(k)
    for j in range(1, local):
        hidden(0, j)
    for p in range(HALVES):
        project(0, po, p)

    def frames_across():
        there = fs[block(z, 1 - y), second_half].astype(F32)
        here = fs[block(z, y), second_half].astype(F32)
        for d in range(outer - 1):
            gz_got(d).wait_recv()
            start = pl.multiple_of(d * INNER * rows, rows)
            there += gz[pl.ds(start + (1 - y) * rows, rows), :].astype(F32)
            here += gz[pl.ds(start + y * rows, rows), :].astype(F32)
        ga[...] = there.astype(BF)
        gy_copy().start()
        fr[:, second_half] = here

    def pass_on(k):
        zo = goal(k)
        for p in range(HALVES):
            my_copy(zo, p).wait_recv()
            here = (zrows(zo), cols_of(p))
            ma[here] = (po[here].astype(F32) + my[here].astype(F32)).astype(BF)
            mz_copy(zo, p).start()

    def finish_frames():
        for d in range(outer - 1):
            fz_got(d).wait_recv()
            fr[:, first_half] += fz[zrows(d), :].astype(F32)
        gy_copy().wait_recv()
        fr[:, second_half] += gy[...].astype(F32)
        got = [fr[t * sessions:(t + 1) * sessions, :] for t in range(steps)]
        decoded = []
        for t in range(steps):
            total = early[t * sessions:(t + 1) * sessions, :]
            for j in range(t + 1):
                total += tapv[j:j + 1, :] * got[t - j]
            decoded.append(jax.nn.gelu(total).astype(BF))
            new_ref[state_len - steps + t] = got[t].astype(BF)
        samples = dot(jnp.concatenate(decoded, axis=0), usv[...]).astype(BF)
        for t in range(steps):
            wave_ref[:, t, :] = samples[t * sessions:(t + 1) * sessions]

    pass_on(0)
    frames_across()
    for p in range(HALVES):
        my_copy(z, p).start()
    for k in range(1, outer - 1):
        pass_on(k)
    finish_frames()
    for p in range(HALVES):
        my_copy(z, p).wait_recv()
        mine[...] = po[zrows(z), cols_of(p)].astype(F32) + my[zrows(z), cols_of(p)].astype(F32)

        for d in range(1, outer):
            mz_got(d, p).wait_recv()
            mine[...] += mz[zrows(d), cols_of(p)].astype(F32)

        for t in range(steps):
            moe_ref[:, t, p * part_cols:(p + 1) * part_cols] = mine[t * sessions:(t + 1) * sessions, :].astype(BF)

    gy_copy().wait_send()
    for give in gives:
        give.wait_send()
    for d in range(1, n_e):
        tell(d).wait_send()
    for zo in range(outer):
        for p in range(PIECES):
            @pl.when((z + 1 < outer) & (zo <= z))
            def _():
                up(zo, p).wait_send()

            @pl.when((z > 0) & (zo >= z))
            def _():
                down(zo, p).wait_send()

            across(zo, p).wait_send()
        for p in range(HALVES):
            my_copy(zo, p).wait_send()
        fy_copy(zo).wait_send()
    for k in range(outer - 1):
        zo = goal(k)
        fz_copy(zo).wait_send()
        gz_copy(zo).wait_send()
        for p in range(HALVES):
            mz_copy(zo, p).wait_send()


def hand_over(a_ref, b_ref, c_ref, a_out, b_out, c_out, sems):
    copies = [
        pltpu.make_async_copy(src, dst, sems.at[i])
        for i, (src, dst) in enumerate(((a_ref, a_out), (b_ref, b_out), (c_ref, c_out)))
    ]
    for copy in copies:
        copy.start()
    for copy in copies:
        copy.wait()


def exchange(args, w_gate, w_up, w_down, table, experts, books):
    n_e = lax.axis_size("expert")
    outer = n_e // INNER
    sessions, steps, width = args[0].shape
    rows = sessions * steps
    used = 2 * experts + 8 + 2 * books
    lanes = used + -used % LANES
    local, _, units = w_gate.shape
    ff = 2 * units
    channels = table.shape[1]
    wave_rows = n_e * rows
    col_rows = outer * rows
    vm = pltpu.VMEM
    dma = lambda *s: pltpu.SemaphoreType.DMA(s)
    hops = outer - 1
    scratch = [vm(a.shape, a.dtype) for a in args] + [
        vm((wave_rows, width), BF),
        vm((wave_rows, lanes), BF),
        vm((local, width, 2 * ff), BF),
        vm((local * ff, width), BF),
        vm(table.shape, BF),
        vm((wave_rows, table.shape[0]), BF),
        vm((wave_rows, local * ff), BF),
        vm((col_rows, local * 2 * ff), F32),
        vm((rows, channels), F32),
        vm((wave_rows, LANES), F32),
        vm((col_rows, width), BF),
        vm((col_rows, width), BF),
        vm((col_rows, width), BF),
        vm((col_rows, width), BF),
        vm((outer * rows, width), BF),
        vm((rows, width // HALVES), F32),
        vm((wave_rows, channels), BF),
        vm((col_rows, channels // 2), BF),
        vm((col_rows, channels // 2), BF),
        vm((hops * rows, channels // 2), BF),
        vm((hops * INNER * rows, channels // 2), BF),
        vm((rows, channels // 2), BF),
        vm((rows, channels // 2), BF),
        vm((rows, channels), F32),
        dma(len(args)), dma(3 * local + 1), dma(3 * local), dma(3 * local),
        dma(outer * PIECES), dma(outer * PIECES), dma(outer * PIECES), dma(n_e * PIECES),
        dma(n_e - 1), dma(n_e - 1),
        dma(outer * HALVES), dma(outer * HALVES), dma(outer * HALVES), dma(outer * HALVES),
        dma(outer), dma(outer), dma(hops), dma(hops), dma(hops), dma(hops), dma(2),
        pltpu.SemaphoreType.REGULAR, pltpu.SemaphoreType.REGULAR, pltpu.SemaphoreType.REGULAR,
    ]
    any_spec = pl.BlockSpec(memory_space=pl.ANY)
    vm_spec = pl.BlockSpec(memory_space=pltpu.VMEM)
    return pl.pallas_call(
        functools.partial(kernel, n_e, experts, books),
        out_shape=(
            vm((sessions, steps, width), BF),
            vm((sessions, steps, args[8].shape[1]), BF),
            vm(args[5].shape, BF),
        ),
        in_specs=[any_spec] * (len(args) + 4),
        out_specs=(vm_spec, vm_spec, vm_spec),
        scratch_shapes=scratch,
        compiler_params=pltpu.CompilerParams(
            collective_id=0, has_side_effects=True, vmem_limit_bytes=60 * 1024 * 1024
        ),
    )(*args, w_gate, w_up, w_down, table)


def per_device(
    hidden_rows, expert_ids, route_weights, w_gate, w_up, w_down,
    codes, owner_slot, code_table, conv_state, conv_taps, conv_bias, upsample,
):
    n_e = lax.axis_size("expert")
    width = hidden_rows.shape[2]
    experts = n_e * w_gate.shape[0]
    books, shard, channels = code_table.shape
    results = exchange(
        (
            hidden_rows, expert_ids.transpose(1, 2, 0), route_weights.transpose(1, 2, 0), codes,
            owner_slot.reshape(1, -1), conv_state.transpose(1, 0, 2), conv_taps, conv_bias.reshape(1, -1), upsample,
        ),
        w_gate, w_up, w_down.reshape(-1, width), code_table.reshape(books * shard, channels),
        experts, books,
    )
    vm_spec = pl.BlockSpec(memory_space=pltpu.VMEM)
    moe, samples, carried = pl.pallas_call(
        hand_over,
        out_shape=tuple(jax.ShapeDtypeStruct(r.shape, r.dtype) for r in results),
        in_specs=[vm_spec] * 3,
        out_specs=(pl.BlockSpec(memory_space=pl.ANY),) * 3,
        scratch_shapes=[pltpu.SemaphoreType.DMA((3,))],
    )(*[pltpu.with_memory_space_constraint(r, pltpu.VMEM) for r in results])
    return moe, samples, carried.transpose(1, 0, 2)


def solution(mesh):
    rows = P(("groups", "expert", "wave"), None, None)
    placed = (
        rows, rows, rows,
        P("expert", None, "wave"), P("expert", None, "wave"), P("expert", "wave", None),
        rows, P(("groups", "expert", "wave")), P(None, "expert", None), rows, P(), P(), P(),
    )
    return jax.shard_map(
        per_device, mesh=mesh, in_specs=placed, out_specs=(rows, rows, rows), check_vma=False
    )
```

```python
import functools

import jax
import jax.numpy as jnp
from jax import lax
from jax.experimental import pallas as pl
from jax.experimental.pallas import tpu as pltpu
from jax.sharding import PartitionSpec as P

MESH = pl.DeviceIdType.MESH
BF = jnp.bfloat16
F32 = jnp.float32
RADIX = 64
LANES = 128
INNER = 2
HALVES = 2
PIECES = 2


def dot(a, b):
    return jnp.dot(a, b, preferred_element_type=F32)


def kernel(
    n_e, experts, books,
    h_ref, id_ref, rw_ref, co_ref, ow_ref, st_ref, tap_ref, bias_ref, us_ref,
    wg_ref, wu_ref, wd_ref, tab_ref,
    moe_ref, wave_ref, new_ref,
    hv, idv, rwv, cov, owv, stv, tapv, biasv, usv,
    xg, meta, wgu, wdv, tabv, mem, act, acc, early, told, po, pn, my, ma, mz, mine,
    fs, fy, fa, fz, gz, ga, gy, fr,
    in_sem, w_sem, pws, pwr, zus, zds, yss, agr, mes, mer,
    mys, myr, mzs, mzr, fys, fyr, fzs, fzr, gzs, gzr, gys, below, above, aside,
):
    outer = n_e // INNER
    sessions, steps, width = hv.shape
    rows = sessions * steps
    channels = tab_ref.shape[1]
    local, _, units = wg_ref.shape
    ff = 2 * units
    shard = tab_ref.shape[0] // books
    wave_rows = n_e * rows
    col_rows = outer * rows
    e = lax.axis_index("expert")
    w = lax.axis_index("wave")
    z = e // INNER
    y = e % INNER
    peer = 1 - w
    ye = z * INNER + (1 - y)
    low = z < outer // 2

    def remote(src, dst, ssem, rsem, te, tw):
        return pltpu.make_async_remote_copy(
            src_ref=src, dst_ref=dst, send_sem=ssem, recv_sem=rsem,
            device_id={"expert": te, "wave": tw}, device_id_type=MESH,
        )

    barrier = pltpu.get_barrier_semaphore()

    def greet(te, tw):
        pl.semaphore_signal(barrier, inc=1, device_id={"expert": te, "wave": tw}, device_id_type=MESH)

    greet(e, peer)
    greet(ye, w)

    @pl.when(z > 0)
    def _():
        greet(e - INNER, w)

    @pl.when(z < outer - 1)
    def _():
        greet(e + INNER, w)

    firsts = [
        pltpu.make_async_copy(src, dst, in_sem.at[i])
        for i, (src, dst) in enumerate((
            (h_ref, hv), (id_ref, idv), (rw_ref, rwv), (co_ref, cov), (ow_ref, owv),
            (st_ref, stv), (tap_ref, tapv), (bias_ref, biasv), (us_ref, usv),
        ))
    ]
    for copy in firsts[:5]:
        copy.start()

    def gate_at(tw):
        return pl.ds(pl.multiple_of(tw * units, LANES), units)

    def up_at(tw):
        return pl.ds(pl.multiple_of(ff + tw * units, LANES), units)

    def down_at(j, tw):
        return pl.ds(pl.multiple_of(j * ff + tw * units, LANES), units)

    def weights(tw):
        pairs = []
        for j in range(local):
            pairs.append((wg_ref.at[j], wgu.at[j, :, gate_at(tw)]))
            pairs.append((wu_ref.at[j], wgu.at[j, :, up_at(tw)]))
        for j in range(local):
            pairs.append((wd_ref.at[pl.ds(j * units, units), :], wdv.at[down_at(j, tw), :]))
        return pairs

    loads = [
        pltpu.make_async_copy(src, dst, w_sem.at[i]) for i, (src, dst) in enumerate(weights(w))
    ]
    table = pltpu.make_async_copy(tab_ref, tabv, w_sem.at[3 * local])
    gives = [
        remote(src, dst, pws.at[i], pwr.at[i], e, peer) for i, (src, dst) in enumerate(weights(w))
    ]
    takes = [
        remote(src, dst, pws.at[i], pwr.at[i], e, peer) for i, (src, dst) in enumerate(weights(peer))
    ]

    piece_cols = width // PIECES

    def at(rel, zo, p):
        return (
            pl.ds(pl.multiple_of((rel * outer + zo) * rows, rows), rows), pl.ds(p * piece_cols, piece_cols)
        )

    def agsem(rel, zo, p):
        return agr.at[(rel * outer + zo) * PIECES + p]

    def up(zo, p):
        s = xg.at[at(0, zo, p)]
        return remote(s, s, zus.at[zo * PIECES + p], agsem(0, zo, p), (z + 1) * INNER + y, w)

    def down(zo, p):
        s = xg.at[at(0, zo, p)]
        return remote(s, s, zds.at[zo * PIECES + p], agsem(0, zo, p), (z - 1) * INNER + y, w)

    def across(zo, p):
        return remote(
            xg.at[at(0, zo, p)], xg.at[at(1, zo, p)], yss.at[zo * PIECES + p], agsem(1, zo, p), ye, w
        )

    def arrived(rel, zo, p):
        s = xg.at[at(rel, zo, p)]
        remote(s, s, yss.at[0], agsem(rel, zo, p), ye, w).wait_recv()

    def meta_at(te, se):
        rel = (te % INNER + se % INNER) % 2
        return pl.ds(pl.multiple_of((rel * outer + se // INNER) * rows, rows), rows)

    def tell(d):
        te = (e + d) % n_e
        return remote(
            meta.at[meta_at(e, e), :], meta.at[meta_at(te, e), :], mes.at[d - 1], mer.at[d - 1], te, w
        )

    def told_by(d):
        se = (e - d + n_e) % n_e
        s = meta.at[meta_at(e, se), :]
        return remote(s, s, mes.at[d - 1], mer.at[d - 1], se, w)

    firsts[0].wait()
    hid = hv[...]
    mine_at = pl.multiple_of(z * rows, rows)
    for t in range(steps):
        xg[pl.ds(mine_at + t * sessions, sessions), :] = hid[:, t, :]
    for copy in firsts[5:]:
        copy.start()
    table.start()
    for load in loads:
        load.start()
    pl.semaphore_wait(barrier, 2 + (z > 0).astype(jnp.int32) + (z < outer - 1).astype(jnp.int32))

    for p in range(PIECES):
        @pl.when(z + 1 < outer)
        def _():
            up(z, p).start()

        @pl.when(z > 0)
        def _():
            down(z, p).start()

        across(z, p).start()
    for give in gives:
        give.start()

    lanes = meta.shape[1]
    dest_at = 2 * experts
    code_at = dest_at + 8

    def placed(count, start):
        here = lax.broadcasted_iota(jnp.int32, (count, lanes), 0)
        there = lax.broadcasted_iota(jnp.int32, (count, lanes), 1)
        return jnp.where(here + start == there, 1.0, 0.0).astype(BF)

    for copy in firsts[1:5]:
        copy.wait()
    owner = owv[...].astype(F32)
    holder = jnp.floor((owner + 0.5) / sessions)
    within = owner - holder * sessions
    holder = jnp.floor((holder + 0.5) / 2)
    expert_i = lax.broadcasted_iota(jnp.int32, (experts, sessions), 0)
    digit = lax.broadcasted_iota(jnp.int32, (8, sessions), 0)
    for t in range(steps):
        both = jnp.zeros((experts, sessions), F32)
        for k in range(idv.shape[1]):
            both += jnp.where(expert_i == idv[t, k:k + 1, :], rwv[t, k:k + 1, :], 0.0)
        high = both.astype(BF).astype(F32)
        dest = holder * rows + t * sessions + within
        top = jnp.floor((dest + 0.5) / RADIX)
        digits = jnp.where(digit == 0, top, jnp.where(digit == 1, dest - top * RADIX, 0.0))
        upright = jnp.concatenate([high, both - high, digits], axis=0).astype(BF)
        extra = lax.dot_general(
            upright, placed(code_at, 0), (((0,), (0,)), ((), ())), preferred_element_type=F32
        )
        co = cov[:, t, :].astype(F32)
        top = jnp.floor((co + 0.5) / RADIX)
        extra += dot(top.astype(BF), placed(books, code_at))
        extra += dot((co - top * RADIX).astype(BF), placed(books, code_at + books))
        meta[pl.ds(mine_at + t * sessions, sessions), :] = extra.astype(BF)

    def signal(sem, te):
        pl.semaphore_signal(sem, inc=1, device_id={"expert": te, "wave": w}, device_id_type=MESH)

    def upward():
        @pl.when(z > 0)
        def _():
            pl.semaphore_wait(below, 1)

        @pl.when(z < outer - 1)
        def _():
            signal(below, e + INNER)

    def downward():
        @pl.when(z < outer - 1)
        def _():
            pl.semaphore_wait(above, 1)

        @pl.when(z > 0)
        def _():
            signal(above, e - INNER)

    @pl.when(low)
    def _():
        upward()
        downward()

    @pl.when(jnp.logical_not(low))
    def _():
        downward()
        upward()

    signal(aside, ye)
    pl.semaphore_wait(aside, 1)
    for d in range(1, n_e):
        tell(d).start()

    for copy in firsts[5:]:
        copy.wait()
    state_len = stv.shape[0]
    taps = tapv.shape[0]

    def before():
        for t in range(steps):
            total = jnp.broadcast_to(biasv[...], (sessions, channels))
            for j in range(t + 1, taps):
                total += tapv[j:j + 1, :] * stv[state_len + t - j].astype(F32)
            early[t * sessions:(t + 1) * sessions, :] = total
        for i in range(state_len - steps):
            new_ref[i] = stv[i + steps]

    def forward(step):
        for p in range(PIECES):
            @pl.when(z - step >= 0)
            def _():
                zo = z - step
                arrived(0, zo, p)

                @pl.when(z + 1 < outer)
                def _():
                    up(zo, p).start()

                across(zo, p).start()

            @pl.when(z + step < outer)
            def _():
                zo = z + step
                arrived(0, zo, p)

                @pl.when(z > 0)
                def _():
                    down(zo, p).start()

                across(zo, p).start()

    src = lax.broadcasted_iota(jnp.int32, (lanes, LANES), 0)
    col = lax.broadcasted_iota(jnp.int32, (lanes, LANES), 1)

    def learn():
        for d in range(1, n_e):
            told_by(d).wait_recv()
        is_code = col < books
        pick = jnp.where(is_code & (src == code_at + col), float(RADIX), 0.0)
        pick += jnp.where(is_code & (src == code_at + books + col), 1.0, 0.0)
        pick += jnp.where((col == books) & (src == dest_at), float(RADIX), 0.0)
        pick += jnp.where((col == books) & (src == dest_at + 1), 1.0, 0.0)
        own = e * local + col - (books + 1)
        is_weight = (col > books) & (col <= books + local)
        pick += jnp.where(is_weight & ((src == own) | (src == own + experts)), 1.0, 0.0)
        told[...] = dot(meta[...], pick.astype(BF))
        lane = lax.broadcasted_iota(jnp.int32, (wave_rows, shard), 1).astype(F32)
        first = (e * shard).astype(F32)
        for q in range(books):
            mem[:, q * shard:(q + 1) * shard] = jnp.where(
                told[:, q:q + 1] - first == lane, 1.0, 0.0
            ).astype(BF)

    def embed():
        place = lax.broadcasted_iota(jnp.int32, (wave_rows, wave_rows), 1).astype(F32)
        order = jnp.where(told[:, books:books + 1] == place, 1.0, 0.0).astype(BF)
        table.wait()
        f_tile = min(channels, 512)

        @pl.loop(0, channels // f_tile)
        def _(n):
            cols = pl.ds(pl.multiple_of(n * f_tile, f_tile), f_tile)
            part = dot(mem[...], tabv[:, cols]).astype(BF)
            fs[:, cols] = lax.dot_general(
                order, part, (((0,), (0,)), ((), ())), preferred_element_type=F32
            ).astype(BF)

    def goal(k):
        if k == outer - 1:
            return z
        down_from = outer - 1 - k
        down_from = down_from - (down_from <= z).astype(jnp.int32)
        up_from = k + (k >= z).astype(jnp.int32)
        return jnp.where(low, down_from, up_from)

    def block(zo, yo):
        return pl.ds(pl.multiple_of((zo * INNER + yo) * rows, rows), rows)

    def zrows(zo):
        return pl.ds(pl.multiple_of(zo * rows, rows), rows)

    def hop(zo):
        return (zo - z + outer) % outer - 1

    split = channels // 2
    first_half = pl.ds(0, split)
    second_half = pl.ds(split, split)

    def pair(zo):
        return pl.ds(pl.multiple_of(zo * INNER * rows, INNER * rows), INNER * rows)

    def fy_copy(zo):
        return remote(fs.at[block(zo, 1 - y), first_half], fy.at[zrows(zo), :], fys.at[zo], fyr.at[zo], ye, w)

    def fz_copy(zo):
        d = hop(zo)
        return remote(fa.at[zrows(zo), :], fz.at[zrows(d), :], fzs.at[d], fzr.at[d], zo * INNER + y, w)

    def fz_got(d):
        s = fz.at[zrows(d), :]
        return remote(s, s, fzs.at[d], fzr.at[d], ye, w)

    def gz_copy(zo):
        d = hop(zo)
        return remote(fs.at[pair(zo), second_half], gz.at[pair(d), :], gzs.at[d], gzr.at[d], zo * INNER + y, w)

    def gz_got(d):
        s = gz.at[pair(d), :]
        return remote(s, s, gzs.at[d], gzr.at[d], ye, w)

    def gy_copy():
        return remote(ga, gy, gys.at[0], gys.at[1], ye, w)

    part_cols = width // HALVES

    def cols_of(p):
        return pl.ds(p * part_cols, part_cols)

    def my_copy(zo, p):
        i = zo * HALVES + p
        return remote(
            pn.at[zrows(zo), cols_of(p)], my.at[zrows(zo), cols_of(p)], mys.at[i], myr.at[i], ye, w
        )

    def mz_copy(zo, p):
        there = (z - zo + outer) % outer
        return remote(
            ma.at[zrows(zo), cols_of(p)], mz.at[zrows(there), cols_of(p)],
            mzs.at[zo * HALVES + p], mzr.at[there * HALVES + p], zo * INNER + y, w,
        )

    def mz_got(there, p):
        s = mz.at[zrows(there), cols_of(p)]
        return remote(s, s, mzs.at[0], mzr.at[there * HALVES + p], ye, w)

    rc = min(col_rows, 128)
    early_cols = width - piece_cols

    def looped(count, body):
        if count == 1:
            body(0)
        else:
            pl.loop(0, count)(body)

    def ready(i):
        loads[i].wait()
        takes[i].wait_recv()

    def hidden(rel, j):
        def piece(i):
            here = pl.ds(pl.multiple_of(rel * col_rows + i * rc, rc), rc)
            x = xg[here, :]
            weight = told[here, books + 1 + j:books + 2 + j]
            tile = ff // 3 if ff % (3 * LANES) == 0 else ff
            for n in range(0, ff, tile):
                g = dot(x, wgu[j, :, n:n + tile])
                u = dot(x, wgu[j, :, ff + n:ff + n + tile])
                a = g / (1.0 + jnp.exp(-g)) * u * weight
                act[here, j * ff + n:j * ff + n + tile] = a.astype(BF)

        looped(col_rows // rc, piece)

    def hidden_start(j):
        def piece(i):
            here = pl.ds(pl.multiple_of(col_rows + i * rc, rc), rc)
            there = pl.ds(pl.multiple_of(i * rc, rc), rc)
            x = xg[here, :early_cols]
            tile = 2 * ff // 3 if ff % (3 * LANES) == 0 else ff
            for n in range(0, 2 * ff, tile):
                acc[there, j * 2 * ff + n:j * 2 * ff + n + tile] = dot(x, wgu[j, :early_cols, n:n + tile])

        looped(col_rows // rc, piece)

    def hidden_end(j):
        def piece(i):
            here = pl.ds(pl.multiple_of(col_rows + i * rc, rc), rc)
            there = pl.ds(pl.multiple_of(i * rc, rc), rc)
            x = xg[here, early_cols:]
            weight = told[here, books + 1 + j:books + 2 + j]
            tile = ff // 3 if ff % (3 * LANES) == 0 else ff
            for n in range(0, ff, tile):
                base = j * 2 * ff + n
                g = acc[there, base:base + tile] + dot(x, wgu[j, early_cols:, n:n + tile])
                u = acc[there, base + ff:base + ff + tile] + dot(x, wgu[j, early_cols:, ff + n:ff + n + tile])
                a = g / (1.0 + jnp.exp(-g)) * u * weight
                act[here, j * ff + n:j * ff + n + tile] = a.astype(BF)

        looped(col_rows // rc, piece)

    def project(rel, dst, p):
        def piece(i):
            here = pl.ds(pl.multiple_of(rel * col_rows + i * rc, rc), rc)
            there = pl.ds(pl.multiple_of(i * rc, rc), rc)
            tile = min(part_cols, 512)
            for n in range(p * part_cols, (p + 1) * part_cols, tile):
                dst[there, n:n + tile] = dot(act[here, :], wdv[:, n:n + tile]).astype(BF)

        looped(col_rows // rc, piece)

    def frames_on(k):
        zo = goal(k)
        total = fs[block(zo, y), first_half].astype(F32)
        fy_copy(zo).wait_recv()
        total += fy[zrows(zo), :].astype(F32)
        if k < outer - 1:
            fa[zrows(zo), :] = total.astype(BF)
            fz_copy(zo).start()
        else:
            fr[:, first_half] = total

    before()
    for step in range(1, outer):
        forward(step)
        if step == min(2, outer - 1):
            learn()
        if step == min(2, outer - 1):
            embed()
    for k in range(outer - 1):
        gz_copy(goal(k)).start()
    for k in range(outer):
        fy_copy(goal(k)).start()

    def both_ready(j):
        ready(2 * j)
        ready(2 * j + 1)

    both_ready(0)
    hidden(0, 0)
    for zo in range(outer):
        for p in range(PIECES - 1):
            arrived(1, zo, p)
    for j in range(local):
        if j > 0:
            both_ready(j)
        hidden_start(j)
    for zo in range(outer):
        arrived(1, zo, PIECES - 1)
    for j in range(local):
        hidden_end(j)
        if j < outer - 1:
            frames_on(j)
    for j in range(local):
        ready(2 * local + j)
    for p in range(HALVES):
        project(1, pn, p)
        my_copy(goal(0), p).start()
    for k in range(1, outer - 1):
        for p in range(HALVES):
            my_copy(goal(k), p).start()
    for k in range(min(local, outer - 1), outer):
        frames_on(k)
    for j in range(1, local):
        hidden(0, j)
    for p in range(HALVES):
        project(0, po, p)

    def frames_across():
        there = fs[block(z, 1 - y), second_half].astype(F32)
        here = fs[block(z, y), second_half].astype(F32)
        for d in range(outer - 1):
            gz_got(d).wait_recv()
            start = pl.multiple_of(d * INNER * rows, rows)
            there += gz[pl.ds(start + (1 - y) * rows, rows), :].astype(F32)
            here += gz[pl.ds(start + y * rows, rows), :].astype(F32)
        ga[...] = there.astype(BF)
        gy_copy().start()
        fr[:, second_half] = here

    def pass_on(k):
        zo = goal(k)
        for p in range(HALVES):
            my_copy(zo, p).wait_recv()
            here = (zrows(zo), cols_of(p))
            ma[here] = (po[here].astype(F32) + my[here].astype(F32)).astype(BF)
            mz_copy(zo, p).start()

    def finish_frames():
        for d in range(outer - 1):
            fz_got(d).wait_recv()
            fr[:, first_half] += fz[zrows(d), :].astype(F32)
        gy_copy().wait_recv()
        fr[:, second_half] += gy[...].astype(F32)
        got = [fr[t * sessions:(t + 1) * sessions, :] for t in range(steps)]
        decoded = []
        for t in range(steps):
            total = early[t * sessions:(t + 1) * sessions, :]
            for j in range(t + 1):
                total += tapv[j:j + 1, :] * got[t - j]
            decoded.append(jax.nn.gelu(total).astype(BF))
            new_ref[state_len - steps + t] = got[t].astype(BF)
        samples = dot(jnp.concatenate(decoded, axis=0), usv[...]).astype(BF)
        for t in range(steps):
            wave_ref[:, t, :] = samples[t * sessions:(t + 1) * sessions]

    pass_on(0)
    frames_across()
    for p in range(HALVES):
        my_copy(z, p).start()
    for k in range(1, outer - 1):
        pass_on(k)
    finish_frames()
    for p in range(HALVES):
        my_copy(z, p).wait_recv()
        mine[...] = po[zrows(z), cols_of(p)].astype(F32) + my[zrows(z), cols_of(p)].astype(F32)

        for d in range(1, outer):
            mz_got(d, p).wait_recv()
            mine[...] += mz[zrows(d), cols_of(p)].astype(F32)

        for t in range(steps):
            moe_ref[:, t, p * part_cols:(p + 1) * part_cols] = mine[t * sessions:(t + 1) * sessions, :].astype(BF)

    gy_copy().wait_send()
    for give in gives:
        give.wait_send()
    for d in range(1, n_e):
        tell(d).wait_send()
    for zo in range(outer):
        for p in range(PIECES):
            @pl.when((z + 1 < outer) & (zo <= z))
            def _():
                up(zo, p).wait_send()

            @pl.when((z > 0) & (zo >= z))
            def _():
                down(zo, p).wait_send()

            across(zo, p).wait_send()
        for p in range(HALVES):
            my_copy(zo, p).wait_send()
        fy_copy(zo).wait_send()
    for k in range(outer - 1):
        zo = goal(k)
        fz_copy(zo).wait_send()
        gz_copy(zo).wait_send()
        for p in range(HALVES):
            mz_copy(zo, p).wait_send()


def hand_over(a_ref, b_ref, c_ref, a_out, b_out, c_out, sems):
    copies = [
        pltpu.make_async_copy(src, dst, sems.at[i])
        for i, (src, dst) in enumerate(((a_ref, a_out), (b_ref, b_out), (c_ref, c_out)))
    ]
    for copy in copies:
        copy.start()
    for copy in copies:
        copy.wait()


def exchange(args, w_gate, w_up, w_down, table, experts, books):
    n_e = lax.axis_size("expert")
    outer = n_e // INNER
    sessions, steps, width = args[0].shape
    rows = sessions * steps
    used = 2 * experts + 8 + 2 * books
    lanes = used + -used % LANES
    local, _, units = w_gate.shape
    ff = 2 * units
    channels = table.shape[1]
    wave_rows = n_e * rows
    col_rows = outer * rows
    vm = pltpu.VMEM
    dma = lambda *s: pltpu.SemaphoreType.DMA(s)
    hops = outer - 1
    scratch = [vm(a.shape, a.dtype) for a in args] + [
        vm((wave_rows, width), BF),
        vm((wave_rows, lanes), BF),
        vm((local, width, 2 * ff), BF),
        vm((local * ff, width), BF),
        vm(table.shape, BF),
        vm((wave_rows, table.shape[0]), BF),
        vm((wave_rows, local * ff), BF),
        vm((col_rows, local * 2 * ff), F32),
        vm((rows, channels), F32),
        vm((wave_rows, LANES), F32),
        vm((col_rows, width), BF),
        vm((col_rows, width), BF),
        vm((col_rows, width), BF),
        vm((col_rows, width), BF),
        vm((outer * rows, width), BF),
        vm((rows, width // HALVES), F32),
        vm((wave_rows, channels), BF),
        vm((col_rows, channels // 2), BF),
        vm((col_rows, channels // 2), BF),
        vm((hops * rows, channels // 2), BF),
        vm((hops * INNER * rows, channels // 2), BF),
        vm((rows, channels // 2), BF),
        vm((rows, channels // 2), BF),
        vm((rows, channels), F32),
        dma(len(args)), dma(3 * local + 1), dma(3 * local), dma(3 * local),
        dma(outer * PIECES), dma(outer * PIECES), dma(outer * PIECES), dma(n_e * PIECES),
        dma(n_e - 1), dma(n_e - 1),
        dma(outer * HALVES), dma(outer * HALVES), dma(outer * HALVES), dma(outer * HALVES),
        dma(outer), dma(outer), dma(hops), dma(hops), dma(hops), dma(hops), dma(2),
        pltpu.SemaphoreType.REGULAR, pltpu.SemaphoreType.REGULAR, pltpu.SemaphoreType.REGULAR,
    ]
    any_spec = pl.BlockSpec(memory_space=pl.ANY)
    vm_spec = pl.BlockSpec(memory_space=pltpu.VMEM)
    return pl.pallas_call(
        functools.partial(kernel, n_e, experts, books),
        out_shape=(
            vm((sessions, steps, width), BF),
            vm((sessions, steps, args[8].shape[1]), BF),
            vm(args[5].shape, BF),
        ),
        in_specs=[any_spec] * (len(args) + 4),
        out_specs=(vm_spec, vm_spec, vm_spec),
        scratch_shapes=scratch,
        compiler_params=pltpu.CompilerParams(
            collective_id=0, has_side_effects=True, vmem_limit_bytes=60 * 1024 * 1024
        ),
    )(*args, w_gate, w_up, w_down, table)


def per_device(
    hidden_rows, expert_ids, route_weights, w_gate, w_up, w_down,
    codes, owner_slot, code_table, conv_state, conv_taps, conv_bias, upsample,
):
    n_e = lax.axis_size("expert")
    width = hidden_rows.shape[2]
    experts = n_e * w_gate.shape[0]
    books, shard, channels = code_table.shape
    results = exchange(
        (
            hidden_rows, expert_ids.transpose(1, 2, 0), route_weights.transpose(1, 2, 0), codes,
            owner_slot.reshape(1, -1), conv_state.transpose(1, 0, 2), conv_taps, conv_bias.reshape(1, -1), upsample,
        ),
        w_gate, w_up, w_down.reshape(-1, width), code_table.reshape(books * shard, channels),
        experts, books,
    )
    vm_spec = pl.BlockSpec(memory_space=pltpu.VMEM)
    moe, samples, carried = pl.pallas_call(
        hand_over,
        out_shape=tuple(jax.ShapeDtypeStruct(r.shape, r.dtype) for r in results),
        in_specs=[vm_spec] * 3,
        out_specs=(pl.BlockSpec(memory_space=pl.ANY),) * 3,
        scratch_shapes=[pltpu.SemaphoreType.DMA((3,))],
    )(*[pltpu.with_memory_space_constraint(r, pltpu.VMEM) for r in results])
    return moe, samples, carried.transpose(1, 0, 2)


def solution(mesh):
    rows = P(("groups", "expert", "wave"), None, None)
    placed = (
        rows, rows, rows,
        P("expert", None, "wave"), P("expert", None, "wave"), P("expert", "wave", None),
        rows, P(("groups", "expert", "wave")), P(None, "expert", None), rows, P(), P(), P(),
    )
    return jax.shard_map(
        per_device, mesh=mesh, in_specs=placed, out_specs=(rows, rows, rows), check_vma=False
    )
```
